256 devices in a mesh: dp: 8 (over x_hi, y), tm: 4 (over x_lo, core), height: 8 (over z).
Axes of the slice: x: 4 (x_hi: 2, x_lo: 2; x = x_hi * 2 + x_lo), y: 4, z: 8, core: 2. Of those that a mesh axis runs over, the one named last changes fastest.
Arguments:
- queries: bfloat16 [8, 16, 32, 8, 2560], P('dp', 'tm', 'height'), may hold values from -9 to 9
- keys: bfloat16 [8, 16, 32, 8, 2560], P('dp', 'tm', 'height'), may hold values from -9 to 9
- values: bfloat16 [8, 16, 32, 8, 2560], P('dp', 'tm', 'height'), may hold values from -6 to 6
- projection: bfloat16 [2560, 2560], P('dp'), may hold values from -0.125 to 0.125
- d_outputs: bfloat16 [8, 16, 32, 8, 2560], P('dp', 'tm', 'height'), may hold values from -6 to 6
Outputs:
- outputs: bfloat16 [8, 16, 32, 8, 2560], P('dp', 'tm', 'height')
- d_queries: bfloat16 [8, 16, 32, 8, 2560], P('dp', 'tm', 'height')
- d_keys: bfloat16 [8, 16, 32, 8, 2560], P('dp', 'tm', 'height')
- d_values: bfloat16 [8, 16, 32, 8, 2560], P('dp', 'tm', 'height')
The draws below stay inside these ranges and needn't reach their ends.
All inputs are finite; a program needn't handle non-finite values.
Results may differ from the reference program's by a relative error of at most 0.01.
Values may be sent and summed in bfloat16 or wider, within the bound.
No kernel may reach another device: no remote copies, remote signals or barrier semaphores. Data moves between devices by JAX's collectives and lax.ppermute only.
A program may use at most 128 MiB of HBM per device.

```python
import math
import jax
import jax.numpy as jnp
from jax import lax

HEADS = 20
HDIM = 128
DW = 2560
TILE = 2
TWIDE = 4
TILES_W = 2
VIDEOS = 8
FRAMES = 16
ROWS = 32
COLS = 8
QKDIM = 2560
N_TM = 4
N_HEIGHT = 8


def drawn_pair(key):
    seeded = jax.random.fold_in(key, 4111)
    seed_query, seed_key = jax.random.split(seeded, 2)
    full_shape = (VIDEOS, FRAMES, ROWS, COLS, HEADS, HDIM)
    merged_shape = (VIDEOS, FRAMES, ROWS, COLS, HEADS * HDIM)
    query_part = jax.random.truncated_normal(seed_query, -6.0, 6.0, full_shape, jnp.float32).reshape(merged_shape)
    key_part = jax.random.truncated_normal(seed_key, -6.0, 6.0, full_shape, jnp.float32).reshape(merged_shape)
    return (query_part.astype(jnp.bfloat16), key_part.astype(jnp.bfloat16))


def draw_queries(key, part):
    return drawn_pair(key)[0]


def draw_keys(key, part):
    return drawn_pair(key)[1]


def shard_levels(stream_key, extent, shards, smallest, high):
    level, own = 1.0, jax.random.fold_in(stream_key, 6)
    for position, blocks in shards:
        heights = jnp.exp(jax.random.uniform(jax.random.fold_in(own, position), (blocks,), jnp.float32, smallest / len(shards), high / len(shards)))
        level = level * jnp.repeat(heights, extent[position] // blocks).reshape([-1 if axis == position else 1 for axis in range(len(extent))])
    return level


def noise(stream_key, dims, width, reach, shards=(), kind=jnp.bfloat16):
    array = jax.random.normal(stream_key, dims, jnp.float32) * width
    if len(shards) > 0:
        array = shard_levels(stream_key, dims, shards, -0.22, 0.18) * array
    return jnp.clip(array, min=-reach, max=reach).astype(kind)


def setup_inputs(seed: int = 0) -> dict:
    key_list = jax.random.split(jax.random.key(seed), 6)
    return {
        "queries": draw_queries(jax.random.fold_in(key_list[5], 71), 0),
        "keys": draw_keys(jax.random.fold_in(key_list[5], 71), 0),
        "values": noise(key_list[2], (VIDEOS, FRAMES, ROWS, COLS, QKDIM), 1.0, 6.0, ((0, 8), (1, 4), (2, 8))),
        "projection": noise(key_list[3], (QKDIM, DW), QKDIM ** -0.5, 0.125, ((0, 8),)),
        "d_outputs": noise(key_list[4], (VIDEOS, FRAMES, ROWS, COLS, DW), 1.0, 6.0, ((0, 8), (1, 4), (2, 8))),
    }


def window_mask(frame_block, row_block, frame_blocks, row_blocks, tiles_across, tile_len, tile_cols):
    grid_shape = (2, 2, tiles_across, 4, 4, tiles_across)
    query_frame = lax.broadcasted_iota(jnp.int32, grid_shape, 0)
    query_row = lax.broadcasted_iota(jnp.int32, grid_shape, 1)
    query_column = lax.broadcasted_iota(jnp.int32, grid_shape, 2)
    key_frame = lax.broadcasted_iota(jnp.int32, grid_shape, 3)
    key_row = lax.broadcasted_iota(jnp.int32, grid_shape, 4)
    key_column = lax.broadcasted_iota(jnp.int32, grid_shape, 5)
    frame_step = key_frame - query_frame - 1
    row_step = key_row - query_row - 1
    column_step = key_column - query_column
    frame_tile = 2 * frame_block + key_frame - 1
    row_tile = 2 * row_block + key_row - 1
    inside = (jnp.abs(frame_step) <= 1) & (jnp.abs(row_step) <= 1) & (jnp.abs(column_step) <= 1)
    inside = inside & (frame_tile >= 0) & (frame_tile < 2 * frame_blocks)
    inside = inside & (row_tile >= 0) & (row_tile < 2 * row_blocks)
    spread = inside[:, None, :, None, :, None, :, None, :, None, :, None]
    spread = jnp.broadcast_to(spread, (2, tile_len, 2, tile_len, tiles_across, tile_cols, 4, tile_len, 4, tile_len, tiles_across, tile_cols))
    query_count = 4 * tile_len * tile_len * tiles_across * tile_cols
    return spread.reshape(query_count, 4 * query_count)

def attend_forward(query_block, key_ext, value_ext, window):
    query_count = window.shape[0]
    key_count = window.shape[1]
    query_heads = query_block.reshape(query_count, HEADS, HDIM).astype(jnp.float32)
    key_heads = key_ext.reshape(key_count, HEADS, HDIM).astype(jnp.float32)
    value_heads = value_ext.reshape(key_count, HEADS, HDIM).astype(jnp.float32)
    scaling = 1.0 / math.sqrt(HDIM)
    scores = jnp.einsum('qhd,khd->hqk', query_heads, key_heads) * scaling
    masked = jnp.where(window[None], scores, -jnp.inf)
    largest = lax.optimization_barrier(jnp.max(masked, axis=2, keepdims=True))
    weights = jnp.exp(masked - largest)
    soft_weights = (weights / lax.optimization_barrier(jnp.sum(weights, axis=2, keepdims=True))).astype(jnp.bfloat16)
    soft_weights = lax.optimization_barrier(soft_weights)
    attended = jnp.einsum('hqk,khd->qhd', soft_weights.astype(jnp.float32), value_heads)
    return (attended.reshape(query_count, HEADS * HDIM).astype(jnp.bfloat16), soft_weights)

def attend_backward(query_block, key_ext, value_ext, soft_weights, grad_attended):
    query_count = soft_weights.shape[1]
    key_count = soft_weights.shape[2]
    query_heads = query_block.reshape(query_count, HEADS, HDIM).astype(jnp.float32)
    key_heads = key_ext.reshape(key_count, HEADS, HDIM).astype(jnp.float32)
    value_heads = value_ext.reshape(key_count, HEADS, HDIM).astype(jnp.float32)
    grad_heads = grad_attended.reshape(query_count, HEADS, HDIM).astype(jnp.float32)
    scaling = 1.0 / math.sqrt(HDIM)
    weights_wide = soft_weights.astype(jnp.float32)
    grad_weights = jnp.einsum('qhd,khd->hqk', grad_heads, value_heads)
    row_dot = lax.optimization_barrier(jnp.sum(weights_wide * grad_weights, axis=2, keepdims=True))
    grad_scores = (weights_wide * (grad_weights - row_dot) * scaling).astype(jnp.bfloat16)
    grad_scores = lax.optimization_barrier(grad_scores).astype(jnp.float32)
    grad_query = jnp.einsum('hqk,khd->qhd', grad_scores, key_heads).reshape(query_count, HEADS * HDIM).astype(jnp.bfloat16)
    grad_key = jnp.einsum('hqk,qhd->khd', grad_scores, query_heads).reshape(key_count, HEADS * HDIM)
    grad_value = jnp.einsum('hqk,qhd->khd', weights_wide, grad_heads).reshape(key_count, HEADS * HDIM)
    return (grad_query, grad_key, grad_value)

def one_video(operands, projection):
    query_video, key_video, value_video, cotangent = operands
    side = 2 * TILE
    pad_spec = ((TILE, TILE), (TILE, TILE), (0, 0), (0, 0))
    key_padded = jnp.pad(key_video, pad_spec)
    value_padded = jnp.pad(value_video, pad_spec)
    block_count = N_TM * N_HEIGHT
    anchor = jnp.zeros((), jnp.int32)

    def block_slices(index):
        index = index.astype(jnp.int32)
        frame_block = index // N_HEIGHT
        row_block = index % N_HEIGHT
        query_block = lax.dynamic_slice(query_video, (frame_block * side, row_block * side, anchor, anchor), (side, side, COLS, QKDIM))
        key_ext = lax.dynamic_slice(key_padded, (frame_block * side, row_block * side, anchor, anchor), (2 * side, 2 * side, COLS, QKDIM))
        value_ext = lax.dynamic_slice(value_padded, (frame_block * side, row_block * side, anchor, anchor), (2 * side, 2 * side, COLS, QKDIM))
        window = window_mask(frame_block, row_block, N_TM, N_HEIGHT, TILES_W, TILE, TWIDE)
        return (query_block, key_ext, value_ext, window)

    def forward_block(index):
        query_block, key_ext, value_ext, window = block_slices(index)
        return attend_forward(query_block, key_ext, value_ext, window)
    block_ids = jnp.arange(block_count, dtype=jnp.int32)
    attended_blocks, weight_blocks = lax.map(forward_block, block_ids)
    attended = attended_blocks.reshape(N_TM, N_HEIGHT, side, side, COLS, QKDIM).transpose(0, 2, 1, 3, 4, 5)
    attended = attended.reshape(FRAMES * ROWS * COLS, QKDIM)
    outputs = jnp.dot(attended, projection, preferred_element_type=jnp.float32).astype(jnp.bfloat16)
    grad_attended = jnp.dot(cotangent.reshape(FRAMES * ROWS * COLS, DW), projection.T, preferred_element_type=jnp.float32).astype(jnp.bfloat16)
    grad_blocks = grad_attended.reshape(N_TM, side, N_HEIGHT, side, COLS, QKDIM).transpose(0, 2, 1, 3, 4, 5)
    grad_blocks = grad_blocks.reshape(block_count, side * side * COLS, QKDIM)

    def backward_block(block_items):
        index, soft_weights, grad_block = block_items
        query_block, key_ext, value_ext, window = block_slices(index)
        grad_query, grad_key, grad_value = attend_backward(query_block, key_ext, value_ext, soft_weights, grad_block)
        stacked = jnp.stack((grad_key, grad_value)).reshape(2, 2 * side, 2 * side, COLS, QKDIM)
        frame_pos = lax.broadcasted_iota(jnp.int32, stacked.shape, 1)
        row_pos = lax.broadcasted_iota(jnp.int32, stacked.shape, 2)
        center = (frame_pos >= TILE) & (frame_pos < 3 * TILE) & (row_pos >= TILE) & (row_pos < 3 * TILE)
        rounded = lax.optimization_barrier(stacked.astype(jnp.bfloat16)).astype(jnp.float32)
        return (grad_query, jnp.where(center, stacked, rounded))
    query_grads, partials = lax.map(backward_block, (block_ids, weight_blocks, grad_blocks))

    def add_block(index, running):
        index = index.astype(jnp.int32)
        frame_block = index // N_HEIGHT
        row_block = index % N_HEIGHT
        start = (anchor, frame_block * side, row_block * side, anchor, anchor)
        current = lax.dynamic_slice(running, start, (2, 2 * side, 2 * side, COLS, QKDIM))
        return lax.dynamic_update_slice(running, current + partials[index], start)
    running = jnp.zeros((2, FRAMES + 2 * TILE, ROWS + 2 * TILE, COLS, QKDIM), jnp.float32)
    running = lax.fori_loop(0, block_count, add_block, running)
    gradients = running[:, TILE:TILE + FRAMES, TILE:TILE + ROWS].astype(jnp.bfloat16)
    d_queries = query_grads.reshape(N_TM, N_HEIGHT, side, side, COLS, QKDIM).transpose(0, 2, 1, 3, 4, 5)
    d_queries = d_queries.reshape(FRAMES, ROWS, COLS, QKDIM)
    return (outputs.reshape(FRAMES, ROWS, COLS, DW), d_queries, gradients[0], gradients[1])

def reference(queries, keys, values, projection, d_outputs):

    def per_video(operands):
        return one_video(operands, projection)
    return lax.map(per_video, (queries, keys, values, d_outputs))
```

```python
import functools
import math

import jax
import jax.numpy as jnp
from jax import lax
from jax.experimental import pallas as pl
from jax.experimental.pallas import tpu as pltpu
from jax.sharding import PartitionSpec as P

HDIM = 128
AXES = ("dp", "tm", "height")
NEG = -1e30
SCALE = 1.0 / math.sqrt(HDIM)
EXP2_SCALE = SCALE * math.log2(math.e)
F32 = jnp.float32
BF16 = jnp.bfloat16

HPS = 2
HEADS_HALF = 10
W_HALF = 1280
VMEM_LIMIT = 10 * 1024 * 1024


def make_perm(shape, fn):
    n_dp, n_tm, n_h = shape
    pairs = []
    for d in range(n_dp):
        for t in range(n_tm):
            for h in range(n_h):
                e, u, g = fn(d, t, h)
                if 0 <= u < n_tm and 0 <= g < n_h:
                    pairs.append(((d * n_tm + t) * n_h + h, (e * n_tm + u) * n_h + g))
    return pairs


def dot(a, b, ca, cb):
    return lax.dot_general(a, b, (((ca,), (cb,)), ((), ())), preferred_element_type=F32)


def in_vmem(shape, dtype):
    return pltpu.VMEM(shape, dtype)


def call(kernel, outs, ins, flops=0, moved=1_000_000, exps=0, scratch=(), aliases=None, hbm_in=0):
    vm = pl.BlockSpec(memory_space=pltpu.VMEM)
    hb = pl.BlockSpec(memory_space=pl.ANY)
    near = [pltpu.with_memory_space_constraint(x, pltpu.VMEM) for x in ins[: len(ins) - hbm_in]]
    far = list(ins[len(ins) - hbm_in :])
    out_specs = [hb if isinstance(o, jax.ShapeDtypeStruct) else vm for o in outs]
    return pl.pallas_call(
        kernel,
        out_shape=tuple(outs),
        in_specs=[vm] * len(near) + [hb] * len(far),
        out_specs=tuple(out_specs),
        scratch_shapes=list(scratch),
        input_output_aliases=aliases or {},
        compiler_params=pltpu.CompilerParams(vmem_limit_bytes=VMEM_LIMIT),
        cost_estimate=pl.CostEstimate(flops=flops, bytes_accessed=moved, transcendentals=exps),
    )(*near, *far)


def half_of(kind):
    mine = lax.axis_index("dp") // 4
    return mine if kind == "local" else 1 - mine


def window_bias(zb_ref, tb_ref):
    tm = lax.axis_index("tm")
    ht = lax.axis_index("height")
    t_lo = jnp.where(tm > 0, 1, 0)
    t_hi = jnp.where(tm < lax.axis_size("tm") - 1, 1, 0)
    z_lo = jnp.where(ht > 0, 1, 0)
    z_hi = jnp.where(ht < lax.axis_size("height") - 1, 1, 0)
    q = lax.broadcasted_iota(jnp.int32, (128, 128), 0)
    k = lax.broadcasted_iota(jnp.int32, (128, 128), 1)
    late = (q // 16) % 2
    side_ok = jnp.where(late == 0, z_lo, z_hi)
    z_side = jnp.where(k < 64, 0, 1)
    zb_ref[...] = jnp.where((z_side == late) & (side_ok > 0), 0.0, NEG).astype(F32)
    t_ok = jnp.where(q < 64, t_lo, t_hi)
    corner = jnp.where(k < 96, 0, 1)
    t_in = (k < 64) | ((corner == late) & (side_ok > 0))
    tb_ref[...] = jnp.where(t_in & (t_ok > 0), 0.0, NEG).astype(F32)


def key_values(k_ref, v_ref, zl_ref, zh_ref, tl_ref, cl_ref, th_ref, ch_ref, c):
    cat = lambda *a: jnp.concatenate(a, axis=0)
    k_oz = cat(k_ref[:, c], zl_ref[0, :, c], zh_ref[0, :, c])
    v_oz = cat(v_ref[:, c], zl_ref[1, :, c], zh_ref[1, :, c])
    k_tl = cat(tl_ref[0, :, c], cl_ref[0, :, c])
    v_tl = cat(tl_ref[1, :, c], cl_ref[1, :, c])
    k_th = cat(th_ref[0, :, c], ch_ref[0, :, c])
    v_th = cat(th_ref[1, :, c], ch_ref[1, :, c])
    return k_oz, v_oz, k_tl, v_tl, k_th, v_th


def lanes(head):
    return pl.ds(pl.multiple_of(head * HDIM, HDIM), HDIM)


def forward_kernel(kind, q_ref, k_ref, v_ref, *rest):
    halo, (att_ref, p_ref, zb_ref, tb_ref) = rest[:6], rest[6:]
    window_bias(zb_ref, tb_ref)
    first = half_of(kind) * HEADS_HALF

    def one(h):
        c = lanes(first + h)
        q = q_ref[:, c]
        k_oz, v_oz, k_tl, v_tl, k_th, v_th = key_values(k_ref, v_ref, *halo, c)
        s_oz = dot(q, k_oz, 1, 1)
        s_t = jnp.concatenate([dot(q[:64], k_tl, 1, 1), dot(q[64:], k_th, 1, 1)], axis=0)
        s_o = s_oz[:, :128]
        s_z = s_oz[:, 128:] + zb_ref[...]
        s_t = s_t + tb_ref[...]
        m = jnp.max(jnp.maximum(jnp.maximum(s_o, s_z), s_t), axis=1, keepdims=True)
        e_o = jnp.exp2((s_o - m) * EXP2_SCALE)
        e_z = jnp.exp2((s_z - m) * EXP2_SCALE)
        e_t = jnp.exp2((s_t - m) * EXP2_SCALE)
        inv = 1.0 / jnp.sum(e_o + e_z + e_t, axis=1, keepdims=True)
        p_oz = jnp.concatenate([e_o * inv, e_z * inv], axis=1).astype(BF16)
        p_t = (e_t * inv).astype(BF16)
        p_ref[h, :, :256] = p_oz
        p_ref[h, :, 256:] = p_t
        a_t = jnp.concatenate([dot(p_t[:64], v_tl, 1, 0), dot(p_t[64:], v_th, 1, 0)], axis=0)
        att_ref[:, lanes(h)] = (dot(p_oz, v_oz, 1, 0) + a_t).astype(BF16)

    def step(i, carry):
        for j in range(HPS):
            one(i * HPS + j)
        return carry

    lax.fori_loop(0, HEADS_HALF // HPS, step, 0)


def forward_half(kind, operands):
    return call(
        functools.partial(forward_kernel, kind),
        (in_vmem((128, W_HALF), BF16), in_vmem((HEADS_HALF, 128, 384), BF16)),
        operands, flops=2 * 2 * 10 * 128 * 384 * 128, moved=6_000_000, exps=10 * 128 * 384,
        scratch=(pltpu.VMEM((128, 128), F32), pltpu.VMEM((128, 128), F32)),
    )


def backward_kernel(kind, q_ref, k_ref, v_ref, *rest):
    halo, (p_ref, g_ref, dq_ref, own_ref, rim_ref, tlo_ref, thi_ref) = rest[:6], rest[6:]
    first = half_of(kind) * HEADS_HALF

    def one(h):
        c = lanes(first + h)
        o = lanes(h)
        q = q_ref[:, c]
        g = g_ref[:, o]
        k_oz, v_oz, k_tl, v_tl, k_th, v_th = key_values(k_ref, v_ref, *halo, c)
        p_oz = p_ref[h, :, :256]
        p_t = p_ref[h, :, 256:]
        dp_oz = dot(g, v_oz, 1, 1)
        dp_t = jnp.concatenate([dot(g[:64], v_tl, 1, 1), dot(g[64:], v_th, 1, 1)], axis=0)
        w_oz = p_oz.astype(F32)
        w_t = p_t.astype(F32)
        x_oz = w_oz * dp_oz
        row = jnp.sum(x_oz[:, :128] + x_oz[:, 128:] + w_t * dp_t, axis=1, keepdims=True)
        ds_oz = (w_oz * (dp_oz - row) * SCALE).astype(BF16)
        ds_t = (w_t * (dp_t - row) * SCALE).astype(BF16)
        dq_t = jnp.concatenate([dot(ds_t[:64], k_tl, 1, 0), dot(ds_t[64:], k_th, 1, 0)], axis=0)
        dq_ref[:, o] = (dot(ds_oz, k_oz, 1, 0) + dq_t).astype(BF16)
        dk_oz = dot(ds_oz, q, 0, 0)
        dv_oz = dot(p_oz, g, 0, 0)
        own_ref[0, :, o] = dk_oz[:128]
        own_ref[1, :, o] = dv_oz[:128]
        rim_ref[0, :, o] = dk_oz[128:]
        rim_ref[1, :, o] = dv_oz[128:]
        tlo_ref[0, :, o] = dot(ds_t[:64], q[:64], 0, 0).astype(BF16)
        tlo_ref[1, :, o] = dot(p_t[:64], g[:64], 0, 0).astype(BF16)
        thi_ref[0, :, o] = dot(ds_t[64:], q[64:], 0, 0).astype(BF16)
        thi_ref[1, :, o] = dot(p_t[64:], g[64:], 0, 0).astype(BF16)

    def step(i, carry):
        for j in range(HPS):
            one(i * HPS + j)
        return carry

    lax.fori_loop(0, HEADS_HALF // HPS, step, 0)


def backward_half(kind, operands, probs, grad):
    pair = (2, 128, W_HALF)
    return call(
        functools.partial(backward_kernel, kind),
        (in_vmem((128, W_HALF), BF16), in_vmem(pair, F32), in_vmem(pair, F32),
         in_vmem(pair, BF16), in_vmem(pair, BF16)),
        (*operands, probs, grad), flops=4 * 2 * 10 * 128 * 384 * 128, moved=12_000_000,
    )


def shard_rows(which):
    y = lax.axis_index("dp") % 4
    core = lax.axis_index("tm") % 2
    toward = jnp.where(core == 0, 3, 1)
    shard = {"own": y, "near": (y + toward) % 4, "far": (y + 4 - toward) % 4}.get(which, (y + 2) % 4)
    at = shard * 320
    if which == "c0":
        at = at + core * 160
    if which == "c1":
        at = at + (1 - core) * 160
    return at


def put_rows(dst_ref, src_ref, which):
    rows = src_ref.shape[0]
    at = shard_rows(which)

    def step(i, carry):
        r = pl.multiple_of(i * 32, 32)
        dst_ref[pl.ds(pl.multiple_of(at + r, 32), 32), :] = src_ref[pl.ds(r, 32), :]
        return carry

    lax.fori_loop(0, rows // 32, step, 0)


def gather_kernel(own_ref, near_ref, far_ref, w_ref):
    put_rows(w_ref, own_ref, "own")
    put_rows(w_ref, near_ref, "near")
    put_rows(w_ref, far_ref, "far")


def gather_rows(own, near, far):
    return call(gather_kernel, (in_vmem((W_HALF, 2560), BF16),), (own, near, far), moved=10_000_000)[0]


def grad_proj_kernel(w_in, c0_ref, c1_ref, mine_ref, theirs_ref, w_ref, o_ref, t_ref):
    put_rows(w_ref, c0_ref, "c0")
    put_rows(w_ref, c1_ref, "c1")

    def step(n, carry):
        r = pl.ds(pl.multiple_of(n * 256, 256), 256)
        w = w_ref[r, :]
        o_ref[:, r] = dot(mine_ref[...], w, 1, 1).astype(BF16)
        t_ref[:, r] = dot(theirs_ref[...], w, 1, 1).astype(BF16)
        return carry

    lax.fori_loop(0, W_HALF // 256, step, 0)


def grad_proj(w, c0, c1, mine, theirs):
    return call(
        grad_proj_kernel,
        (in_vmem((W_HALF, 2560), BF16), in_vmem((128, W_HALF), BF16), in_vmem((128, W_HALF), BF16)),
        (w, c0, c1, mine, theirs), flops=2 * 256 * 1280 * 2560, moved=9_000_000, aliases={0: 0},
    )


def out_proj_kernel(w_ref, mine_ref, theirs_ref, o_ref, t_ref):
    def step(n, carry):
        r = pl.ds(pl.multiple_of(n * 256, 256), 256)
        w = w_ref[:, r]
        o_ref[:, r] = dot(mine_ref[...], w, 1, 0)
        t_ref[:, r] = dot(theirs_ref[...], w, 1, 0).astype(BF16)
        return carry

    lax.fori_loop(0, 2560 // 256, step, 0)


def out_proj(w, mine, theirs):
    return call(
        out_proj_kernel, (in_vmem((128, 2560), F32), in_vmem((128, 2560), BF16)),
        (w, mine, theirs), flops=2 * 256 * 1280 * 2560, moved=9_000_000,
    )


def rim_kernel(rim_ref, prev_ref, next_ref, lo_ref, hi_ref):
    for half, out in ((0, lo_ref), (1, hi_ref)):
        c = slice(64 + 32 * half, 96 + 32 * half)
        corner = jnp.concatenate([prev_ref[:, c], next_ref[:, c]], axis=1).astype(F32)
        out[...] = (rim_ref[:, 64 * half : 64 * half + 64] + corner).astype(BF16)


def rim_half(rim, from_prev, from_next):
    return call(
        rim_kernel, (in_vmem((2, 64, W_HALF), BF16),) * 2, (rim, from_prev, from_next),
        moved=4_000_000,
    )


def final_kernel(kind, own_ref, prev_ref, next_ref, lo_ref, hi_ref, d_ref, *rest):
    dk_ref, dv_ref, dq_ref, dk_tile, dv_tile, sems = rest[-6:]
    at = pl.ds(pl.multiple_of(half_of(kind) * W_HALF, W_HALF), W_HALF)
    copies = [pltpu.make_async_copy(d_ref, dq_ref.at[:, at], sems.at[2])]
    copies[0].start()
    for kv, tile, out in ((0, dk_tile, dk_ref), (1, dv_tile, dv_ref)):
        frames = jnp.concatenate([prev_ref[kv, :64], next_ref[kv, :64]], axis=0).astype(F32)
        total = own_ref[kv] + frames
        for f in range(4):
            low = total[f * 32 : f * 32 + 16] + lo_ref[kv, f * 16 : f * 16 + 16].astype(F32)
            high = total[f * 32 + 16 : f * 32 + 32] + hi_ref[kv, f * 16 : f * 16 + 16].astype(F32)
            tile[f * 32 : f * 32 + 16] = low.astype(BF16)
            tile[f * 32 + 16 : f * 32 + 32] = high.astype(BF16)
        copies.append(pltpu.make_async_copy(tile, out.at[:, at], sems.at[kv]))
        copies[-1].start()
    for cp in copies:
        cp.wait()


def final_half(kind, own, from_prev, from_next, from_lo, from_hi, d_q, *earlier):
    whole = jax.ShapeDtypeStruct((128, 2560), BF16)
    return call(
        functools.partial(final_kernel, kind), (whole,) * 3,
        (own, from_prev, from_next, from_lo, from_hi, d_q, *earlier), moved=6_000_000,
        scratch=(pltpu.VMEM((128, W_HALF), BF16), pltpu.VMEM((128, W_HALF), BF16), pltpu.SemaphoreType.DMA((3,))),
        aliases={6: 0, 7: 1, 8: 2} if earlier else {}, hbm_in=len(earlier),
    )


def prep_kernel(k_ref, v_ref, zlo_ref, zhi_ref, tlo_ref, thi_ref):
    for kv, src in ((0, k_ref), (1, v_ref)):
        for f in range(4):
            zlo_ref[kv, f * 16 : f * 16 + 16] = src[f * 32 : f * 32 + 16]
            zhi_ref[kv, f * 16 : f * 16 + 16] = src[f * 32 + 16 : f * 32 + 32]
        tlo_ref[kv] = src[:64]
        thi_ref[kv] = src[64:]


def prep(keys, values):
    return call(prep_kernel, (in_vmem((2, 64, 2560), BF16),) * 4, (keys, values), moved=4_000_000)


def corner_kernel(lo_ref, hi_ref, down_ref, up_ref):
    down_ref[:, :32] = lo_ref[:, :32]
    down_ref[:, 32:] = hi_ref[:, :32]
    up_ref[:, :32] = lo_ref[:, 32:]
    up_ref[:, 32:] = hi_ref[:, 32:]


def corners(z_lo, z_hi):
    return call(corner_kernel, (in_vmem((2, 64, 2560), BF16),) * 2, (z_lo, z_hi), moved=2_600_000)


def body(queries, keys, values, projection, d_outputs):
    shape = (lax.axis_size("dp"), lax.axis_size("tm"), lax.axis_size("height"))

    def send(x, fn):
        return lax.ppermute(x, AXES, make_perm(shape, fn))

    pair_chip = lambda d, t, h: (d ^ 4, t ^ 2, h)
    other_core = lambda d, t, h: (d, t ^ 1, h)
    ring_y = lambda d, t, h: ((d & 4) | ((d + (1 if t % 2 == 0 else 3)) & 3), t, h)
    up_z = lambda d, t, h: (d, t, h + 1)
    down_z = lambda d, t, h: (d, t, h - 1)
    up_t = lambda d, t, h: (d, t + 1, h)
    down_t = lambda d, t, h: (d, t - 1, h)

    tokens = queries.shape[1] * queries.shape[2] * queries.shape[3]
    flat = lambda a: a.reshape(tokens, a.shape[-1])
    q, k, v, d_out = flat(queries), flat(keys), flat(values), flat(d_outputs)

    w_near = send(projection, ring_y)
    their_d_out = send(d_out, pair_chip)
    z_lo_s, z_hi_s, t_lo_s, t_hi_s = prep(k, v)
    z_lo = send(z_hi_s, up_z)
    z_hi = send(z_lo_s, down_z)
    t_lo = send(t_hi_s, up_t)
    t_hi = send(t_lo_s, down_t)
    c_down, c_up = corners(z_lo, z_hi)
    c_lo = send(c_up, up_t)
    c_hi = send(c_down, down_t)
    w_far = send(w_near, other_core)
    core = lax.axis_index("tm") % 2
    w_c0 = send(lax.dynamic_slice_in_dim(w_near, core * 160, 160, 0), ring_y)
    w_c1 = send(w_c0, other_core)
    rows = gather_rows(projection, w_near, w_far)

    operands = (q, k, v, z_lo, z_hi, t_lo, c_lo, t_hi, c_hi)
    att_remote, p_remote = forward_half("remote", operands)
    their_att = send(att_remote, pair_chip)
    att_local, p_local = forward_half("local", operands)

    rows, g_local, g_theirs = grad_proj(rows, w_c0, w_c1, d_out, their_d_out)
    g_remote = send(g_theirs, pair_chip)

    dq_a, own_a, rim_a, tlo_a, thi_a = backward_half("local", operands, p_local, g_local)
    prev_a = send(thi_a, up_t)
    next_a = send(tlo_a, down_t)
    dq_b, own_b, rim_b, tlo_b, thi_b = backward_half("remote", operands, p_remote, g_remote)
    prev_b = send(thi_b, up_t)
    next_b = send(tlo_b, down_t)

    part, part_theirs = out_proj(rows, att_local, their_att)
    part_remote = send(part_theirs, pair_chip)

    rlo_a, rhi_a = rim_half(rim_a, prev_a, next_a)
    from_lo_a = send(rhi_a, up_z)
    from_hi_a = send(rlo_a, down_z)
    rlo_b, rhi_b = rim_half(rim_b, prev_b, next_b)
    from_lo_b = send(rhi_b, up_z)
    from_hi_b = send(rlo_b, down_z)

    outputs = (part + part_remote.astype(F32)).astype(BF16)
    done = final_half("local", own_a, prev_a, next_a, from_lo_a, from_hi_a, dq_a)
    dk, dv, dq = final_half("remote", own_b, prev_b, next_b, from_lo_b, from_hi_b, dq_b, *done)
    return (
        outputs.reshape(d_outputs.shape),
        dq.reshape(queries.shape),
        dk.reshape(keys.shape),
        dv.reshape(values.shape),
    )


def solution(mesh):
    spec = P("dp", "tm", "height", None, None)
    return jax.shard_map(
        body, mesh=mesh, in_specs=(spec, spec, spec, P("dp", None), spec),
        out_specs=(spec, spec, spec, spec), check_vma=False,
    )
```

```python
import functools
import math

import jax
import jax.numpy as jnp
from jax import lax
from jax.experimental import pallas as pl
from jax.experimental.pallas import tpu as pltpu
from jax.sharding import PartitionSpec as P

HDIM = 128
AXES = ("dp", "tm", "height")
NEG = -1e30
SCALE = 1.0 / math.sqrt(HDIM)
EXP2_SCALE = SCALE * math.log2(math.e)
F32 = jnp.float32
BF16 = jnp.bfloat16

HPS = 2
HEADS_HALF = 10
W_HALF = 1280
VMEM_LIMIT = 10 * 1024 * 1024


def make_perm(shape, fn):
    n_dp, n_tm, n_h = shape
    pairs = []
    for d in range(n_dp):
        for t in range(n_tm):
            for h in range(n_h):
                e, u, g = fn(d, t, h)
                pairs.append(((d * n_tm + t) * n_h + h, (e * n_tm + u) * n_h + g % n_h))
    return pairs


def dot(a, b, ca, cb):
    return lax.dot_general(a, b, (((ca,), (cb,)), ((), ())), preferred_element_type=F32)


def in_vmem(shape, dtype):
    return pltpu.VMEM(shape, dtype)


def call(kernel, outs, ins, flops=0, moved=1_000_000, exps=0, scratch=(), aliases=None, hbm_in=0):
    vm = pl.BlockSpec(memory_space=pltpu.VMEM)
    hb = pl.BlockSpec(memory_space=pl.ANY)
    near = [pltpu.with_memory_space_constraint(x, pltpu.VMEM) for x in ins[: len(ins) - hbm_in]]
    far = [pltpu.with_memory_space_constraint(x, pltpu.HBM) for x in ins[len(ins) - hbm_in :]]
    out_specs = [hb if isinstance(o, jax.ShapeDtypeStruct) else vm for o in outs]
    return pl.pallas_call(
        kernel,
        out_shape=tuple(outs),
        in_specs=[vm] * len(near) + [pl.BlockSpec(memory_space=pltpu.HBM)] * len(far),
        out_specs=tuple(out_specs),
        scratch_shapes=list(scratch),
        input_output_aliases=aliases or {},
        compiler_params=pltpu.CompilerParams(vmem_limit_bytes=VMEM_LIMIT),
        cost_estimate=pl.CostEstimate(flops=flops, bytes_accessed=moved, transcendentals=exps),
    )(*near, *far)


def half_of(kind):
    mine = lax.axis_index("dp") // 4
    return mine if kind == "local" else 1 - mine


def side_rows(side, count=64):
    core = lax.axis_index("tm") % 2
    at = core * count if side == "x" else (1 - core) * count
    return pl.multiple_of(at, count)


def window_bias(zb_ref, tb_ref):
    tm = lax.axis_index("tm")
    ht = lax.axis_index("height")
    last = lax.axis_size("tm") - 1
    x_ok = jnp.where((tm > 0) & (tm < last), 1, 0)
    z_lo = jnp.where(ht > 0, 1, 0)
    z_hi = jnp.where(ht < lax.axis_size("height") - 1, 1, 0)
    q = lax.broadcasted_iota(jnp.int32, (128, 128), 0)
    k = lax.broadcasted_iota(jnp.int32, (128, 128), 1)
    late = (q // 16) % 2
    side_ok = jnp.where(late == 0, z_lo, z_hi)
    z_side = jnp.where(k < 64, 0, 1)
    zb_ref[...] = jnp.where((z_side == late) & (side_ok > 0), 0.0, NEG).astype(F32)
    t_ok = jnp.where(q < 64, x_ok, 1)
    corner = jnp.where(k < 96, 0, 1)
    t_in = (k < 64) | ((corner == late) & (side_ok > 0))
    tb_ref[...] = jnp.where(t_in & (t_ok > 0), 0.0, NEG).astype(F32)


def key_values(k_ref, v_ref, zl_ref, zh_ref, tx_ref, cx_ref, tc_ref, cc_ref, c):
    cat = lambda *a: jnp.concatenate(a, axis=0)
    k_oz = cat(k_ref[:, c], zl_ref[0, :, c], zh_ref[0, :, c])
    v_oz = cat(v_ref[:, c], zl_ref[1, :, c], zh_ref[1, :, c])
    k_tx = cat(tx_ref[0, :, c], cx_ref[0, :, c])
    v_tx = cat(tx_ref[1, :, c], cx_ref[1, :, c])
    k_tc = cat(tc_ref[0, :, c], cc_ref[0, :, c])
    v_tc = cat(tc_ref[1, :, c], cc_ref[1, :, c])
    return k_oz, v_oz, k_tx, v_tx, k_tc, v_tc


def both_sides(ref, c):
    return jnp.concatenate(
        [ref[pl.ds(side_rows("x"), 64), c], ref[pl.ds(side_rows("c"), 64), c]], axis=0
    )


def put_sides(ref, c, value):
    ref[pl.ds(side_rows("x"), 64), c] = value[:64]
    ref[pl.ds(side_rows("c"), 64), c] = value[64:]


def lanes(head):
    return pl.ds(pl.multiple_of(head * HDIM, HDIM), HDIM)


def forward_kernel(kind, q_ref, k_ref, v_ref, *rest):
    halo, (att_ref, p_ref, zb_ref, tb_ref) = rest[:6], rest[6:]
    window_bias(zb_ref, tb_ref)
    first = half_of(kind) * HEADS_HALF

    def one(h):
        c = lanes(first + h)
        q = both_sides(q_ref, c)
        k_oz, v_oz, k_tx, v_tx, k_tc, v_tc = key_values(k_ref, v_ref, *halo, c)
        s_oz = dot(q, k_oz, 1, 1)
        s_t = jnp.concatenate([dot(q[:64], k_tx, 1, 1), dot(q[64:], k_tc, 1, 1)], axis=0)
        s_o = s_oz[:, :128]
        s_z = s_oz[:, 128:] + zb_ref[...]
        s_t = s_t + tb_ref[...]
        m = jnp.max(jnp.maximum(jnp.maximum(s_o, s_z), s_t), axis=1, keepdims=True)
        e_o = jnp.exp2((s_o - m) * EXP2_SCALE)
        e_z = jnp.exp2((s_z - m) * EXP2_SCALE)
        e_t = jnp.exp2((s_t - m) * EXP2_SCALE)
        inv = 1.0 / jnp.sum(e_o + e_z + e_t, axis=1, keepdims=True)
        p_oz = jnp.concatenate([e_o * inv, e_z * inv], axis=1).astype(BF16)
        p_t = (e_t * inv).astype(BF16)
        p_ref[h, :, :256] = p_oz
        p_ref[h, :, 256:] = p_t
        a_t = jnp.concatenate([dot(p_t[:64], v_tx, 1, 0), dot(p_t[64:], v_tc, 1, 0)], axis=0)
        put_sides(att_ref, lanes(h), (dot(p_oz, v_oz, 1, 0) + a_t).astype(BF16))

    def step(i, carry):
        for j in range(HPS):
            one(i * HPS + j)
        return carry

    lax.fori_loop(0, HEADS_HALF // HPS, step, 0)


def forward_half(kind, operands):
    return call(
        functools.partial(forward_kernel, kind),
        (in_vmem((128, W_HALF), BF16), in_vmem((HEADS_HALF, 128, 384), BF16)),
        operands, flops=2 * 2 * 10 * 128 * 384 * 128, moved=6_000_000, exps=10 * 128 * 384,
        scratch=(pltpu.VMEM((128, 128), F32), pltpu.VMEM((128, 128), F32)),
    )


def backward_kernel(kind, q_ref, k_ref, v_ref, *rest):
    halo, (p_ref, g_ref, dq_ref, own_ref, rim_ref, tx_ref, tc_ref) = rest[:6], rest[6:]
    first = half_of(kind) * HEADS_HALF

    def one(h):
        c = lanes(first + h)
        o = lanes(h)
        q = both_sides(q_ref, c)
        g = both_sides(g_ref, o)
        k_oz, v_oz, k_tx, v_tx, k_tc, v_tc = key_values(k_ref, v_ref, *halo, c)
        p_oz = p_ref[h, :, :256]
        p_t = p_ref[h, :, 256:]
        dp_oz = dot(g, v_oz, 1, 1)
        dp_t = jnp.concatenate([dot(g[:64], v_tx, 1, 1), dot(g[64:], v_tc, 1, 1)], axis=0)
        w_oz = p_oz.astype(F32)
        w_t = p_t.astype(F32)
        x_oz = w_oz * dp_oz
        row = jnp.sum(x_oz[:, :128] + x_oz[:, 128:] + w_t * dp_t, axis=1, keepdims=True)
        ds_oz = (w_oz * (dp_oz - row) * SCALE).astype(BF16)
        ds_t = (w_t * (dp_t - row) * SCALE).astype(BF16)
        dq_t = jnp.concatenate([dot(ds_t[:64], k_tx, 1, 0), dot(ds_t[64:], k_tc, 1, 0)], axis=0)
        put_sides(dq_ref, o, (dot(ds_oz, k_oz, 1, 0) + dq_t).astype(BF16))
        dk_oz = dot(ds_oz, q, 0, 0)
        dv_oz = dot(p_oz, g, 0, 0)
        own_ref[0, :, o] = dk_oz[:128]
        own_ref[1, :, o] = dv_oz[:128]
        rim_ref[0, :, o] = dk_oz[128:]
        rim_ref[1, :, o] = dv_oz[128:]
        tx_ref[0, :, o] = dot(ds_t[:64], q[:64], 0, 0).astype(BF16)
        tx_ref[1, :, o] = dot(p_t[:64], g[:64], 0, 0).astype(BF16)
        tc_ref[0, :, o] = dot(ds_t[64:], q[64:], 0, 0).astype(BF16)
        tc_ref[1, :, o] = dot(p_t[64:], g[64:], 0, 0).astype(BF16)

    def step(i, carry):
        for j in range(HPS):
            one(i * HPS + j)
        return carry

    lax.fori_loop(0, HEADS_HALF // HPS, step, 0)


def backward_half(kind, operands, probs, grad):
    pair = (2, 128, W_HALF)
    return call(
        functools.partial(backward_kernel, kind),
        (in_vmem((128, W_HALF), BF16), in_vmem(pair, F32), in_vmem(pair, F32),
         in_vmem(pair, BF16), in_vmem(pair, BF16)),
        (*operands, probs, grad), flops=4 * 2 * 10 * 128 * 384 * 128, moved=12_000_000,
    )


def shard_rows(which):
    y = lax.axis_index("dp") % 4
    core = lax.axis_index("tm") % 2
    toward = jnp.where(core == 0, 3, 1)
    shard = {"own": y, "near": (y + toward) % 4, "far": (y + 4 - toward) % 4}.get(which, (y + 2) % 4)
    at = shard * 320
    if which == "c0":
        at = at + core * 160
    if which == "c1":
        at = at + (1 - core) * 160
    return at


def put_rows(dst_ref, src_ref, which):
    rows = src_ref.shape[0]
    at = shard_rows(which)

    def step(i, carry):
        r = pl.multiple_of(i * 32, 32)
        dst_ref[pl.ds(pl.multiple_of(at + r, 32), 32), :] = src_ref[pl.ds(r, 32), :]
        return carry

    lax.fori_loop(0, rows // 32, step, 0)


def gather_kernel(own_ref, near_ref, far_ref, w_ref):
    put_rows(w_ref, own_ref, "own")
    put_rows(w_ref, near_ref, "near")
    put_rows(w_ref, far_ref, "far")


def gather_rows(own, near, far):
    return call(
        gather_kernel, (in_vmem((W_HALF, 2560), BF16),), (own, near, far), moved=10_000_000
    )[0]


def grad_proj_kernel(w_in, c0_ref, c1_ref, mine_ref, theirs_ref, w_ref, o_ref, t_ref):
    put_rows(w_ref, c0_ref, "c0")
    put_rows(w_ref, c1_ref, "c1")

    def step(n, carry):
        r = pl.ds(pl.multiple_of(n * 256, 256), 256)
        w = w_ref[r, :]
        o_ref[:, r] = dot(mine_ref[...], w, 1, 1).astype(BF16)
        t_ref[:, r] = dot(theirs_ref[...], w, 1, 1).astype(BF16)
        return carry

    lax.fori_loop(0, W_HALF // 256, step, 0)


def grad_proj(w, c0, c1, mine, theirs):
    return call(
        grad_proj_kernel,
        (in_vmem((W_HALF, 2560), BF16), in_vmem((128, W_HALF), BF16), in_vmem((128, W_HALF), BF16)),
        (w, c0, c1, mine, theirs), flops=2 * 256 * 1280 * 2560, moved=9_000_000, aliases={0: 0},
    )


def out_proj_kernel(w_ref, mine_ref, theirs_ref, o_ref, t_ref):
    def step(n, carry):
        r = pl.ds(pl.multiple_of(n * 256, 256), 256)
        w = w_ref[:, r]
        o_ref[:, r] = dot(mine_ref[...], w, 1, 0)
        t_ref[:, r] = dot(theirs_ref[...], w, 1, 0).astype(BF16)
        return carry

    lax.fori_loop(0, 2560 // 256, step, 0)


def out_proj(w, mine, theirs):
    return call(
        out_proj_kernel, (in_vmem((128, 2560), F32), in_vmem((128, 2560), BF16)),
        (w, mine, theirs), flops=2 * 256 * 1280 * 2560, moved=9_000_000,
    )


def rim_kernel(rim_ref, fx_ref, fc_ref, lo_ref, hi_ref):
    for side, src in (("x", fx_ref), ("c", fc_ref)):
        at = side_rows(side, 32)
        for half, out in ((0, lo_ref), (1, hi_ref)):
            corner = src[:, 64 + 32 * half : 96 + 32 * half].astype(F32)
            here = rim_ref[:, pl.ds(pl.multiple_of(64 * half + at, 32), 32)]
            out[:, pl.ds(at, 32)] = (here + corner).astype(BF16)


def rim_half(rim, from_x, from_c):
    return call(
        rim_kernel, (in_vmem((2, 64, W_HALF), BF16),) * 2, (rim, from_x, from_c),
        moved=4_000_000,
    )


def final_kernel(kind, own_ref, fx_ref, fc_ref, lo_ref, hi_ref, d_ref, *rest):
    dk_ref, dv_ref, dq_ref, dk_tile, dv_tile, sems = rest[-6:]
    at = pl.ds(pl.multiple_of(half_of(kind) * W_HALF, W_HALF), W_HALF)
    copies = [pltpu.make_async_copy(d_ref, dq_ref.at[:, at], sems.at[2])]
    copies[0].start()
    for kv, tile, out in ((0, dk_tile, dk_ref), (1, dv_tile, dv_ref)):
        for side, src in (("x", fx_ref), ("c", fc_ref)):
            for f in range(2):
                for n, z_ref in ((0, lo_ref), (1, hi_ref)):
                    r = pl.ds(pl.multiple_of(side_rows(side) + f * 32 + n * 16, 16), 16)
                    z = z_ref[kv, pl.ds(pl.multiple_of(side_rows(side, 32) + f * 16, 16), 16)]
                    t = src[kv, f * 32 + n * 16 : f * 32 + n * 16 + 16]
                    tile[r] = (own_ref[kv, r] + t.astype(F32) + z.astype(F32)).astype(BF16)
        copies.append(pltpu.make_async_copy(tile, out.at[:, at], sems.at[kv]))
        copies[-1].start()
    for cp in copies:
        cp.wait()


def final_half(kind, own, from_x, from_c, from_lo, from_hi, d_q, *earlier):
    whole = jax.ShapeDtypeStruct((128, 2560), BF16)
    return call(
        functools.partial(final_kernel, kind), (whole,) * 3,
        (own, from_x, from_c, from_lo, from_hi, d_q, *earlier), moved=6_000_000,
        scratch=(pltpu.VMEM((128, W_HALF), BF16), pltpu.VMEM((128, W_HALF), BF16), pltpu.SemaphoreType.DMA((3,))),
        aliases={6: 0, 7: 1, 8: 2} if earlier else {}, hbm_in=len(earlier),
    )


def prep_kernel(k_ref, v_ref, zlo_ref, zhi_ref, tx_ref, tc_ref, sems):
    copies = []
    for kv, src in ((0, k_ref), (1, v_ref)):
        for f in range(4):
            rows = pl.ds(f * 16, 16)
            copies.append((src.at[pl.ds(f * 32 + 16, 16)], zhi_ref.at[kv, rows]))
            copies.append((src.at[pl.ds(f * 32, 16)], zlo_ref.at[kv, rows]))
    for kv, src in ((0, k_ref), (1, v_ref)):
        copies.append((src.at[pl.ds(side_rows("x"), 64)], tx_ref.at[kv]))
        copies.append((src.at[pl.ds(side_rows("c"), 64)], tc_ref.at[kv]))
    copies = [pltpu.make_async_copy(x, y, sems.at[n]) for n, (x, y) in enumerate(copies)]
    for cp in copies:
        cp.start()
    for cp in copies:
        cp.wait()


def prep(keys, values):
    return call(
        prep_kernel, (in_vmem((2, 64, 2560), BF16),) * 4, (keys, values), moved=4_000_000,
        scratch=(pltpu.SemaphoreType.DMA((20,)),), hbm_in=2,
    )


def slice_kernel(near_ref, part_ref):
    core = lax.axis_index("tm") % 2

    def step(i, carry):
        r = pl.multiple_of(i * 32, 32)
        part_ref[pl.ds(r, 32), :] = near_ref[pl.ds(pl.multiple_of(core * 160 + r, 32), 32), :]
        return carry

    lax.fori_loop(0, 5, step, 0)


def add_kernel(part_ref, remote_ref, out_ref):
    out_ref[...] = (part_ref[...] + remote_ref[...].astype(F32)).astype(BF16)


def corner_kernel(lo_ref, hi_ref, cx_ref, cc_ref):
    for side, out in (("x", cx_ref), ("c", cc_ref)):
        r = pl.ds(side_rows(side, 32), 32)
        out[:, :32] = lo_ref[:, r]
        out[:, 32:] = hi_ref[:, r]


def corners(z_lo, z_hi):
    return call(corner_kernel, (in_vmem((2, 64, 2560), BF16),) * 2, (z_lo, z_hi), moved=2_600_000)


def body(queries, keys, values, projection, d_outputs):
    shape = (lax.axis_size("dp"), lax.axis_size("tm"), lax.axis_size("height"))

    def send(x, fn):
        return lax.ppermute(x, AXES, make_perm(shape, fn))

    pair_chip = lambda d, t, h: (d ^ 4, t ^ 2, h)
    other_core = lambda d, t, h: (d, t ^ 1, h)
    ring_y = lambda d, t, h: ((d & 4) | ((d + (1 if t % 2 == 0 else 3)) & 3), t, h)
    up_z = lambda d, t, h: (d, t, h + 1)
    down_z = lambda d, t, h: (d, t, h - 1)
    other_chip = lambda d, t, h: (d, 3 - t, h) if t in (1, 2) else (d ^ 4, 3 - t, h)
    other_chip_mid = lambda d, t, h: (d, 3 - t, h) if t in (1, 2) else (d, t, h ^ 1)
    other_chip_late = lambda d, t, h: (d, 3 - t, h) if t in (1, 2) else (d ^ 1, t, h)

    tokens = queries.shape[1] * queries.shape[2] * queries.shape[3]
    flat = lambda a: a.reshape(tokens, a.shape[-1])
    q, k, v, d_out = flat(queries), flat(keys), flat(values), flat(d_outputs)

    w_near = send(projection, ring_y)
    their_d_out = send(d_out, pair_chip)
    z_lo_s, z_hi_s, tx_s, tc_s = prep(k, v)
    z_lo = send(z_hi_s, up_z)
    z_hi = send(z_lo_s, down_z)
    t_x = send(tx_s, other_chip)
    t_c = send(tc_s, other_core)
    cx_s, cc_s = corners(z_lo, z_hi)
    c_x = send(cx_s, other_chip_mid)
    c_c = send(cc_s, other_core)
    w_far = send(w_near, other_core)
    (w_part,) = call(slice_kernel, (in_vmem((160, 2560), BF16),), (w_near,))
    w_c0 = send(w_part, ring_y)
    w_c1 = send(w_c0, other_core)
    rows = gather_rows(projection, w_near, w_far)

    operands = (q, k, v, z_lo, z_hi, t_x, c_x, t_c, c_c)
    att_remote, p_remote = forward_half("remote", operands)
    their_att = send(att_remote, pair_chip)
    att_local, p_local = forward_half("local", operands)

    rows, g_local, g_theirs = grad_proj(rows, w_c0, w_c1, d_out, their_d_out)
    g_remote = send(g_theirs, pair_chip)

    dq_a, own_a, rim_a, tx_a, tc_a = backward_half("local", operands, p_local, g_local)
    fx_a = send(tx_a, other_chip_late)
    fc_a = send(tc_a, other_core)
    dq_b, own_b, rim_b, tx_b, tc_b = backward_half("remote", operands, p_remote, g_remote)
    fx_b = send(tx_b, other_chip_late)
    fc_b = send(tc_b, other_core)

    part, part_theirs = out_proj(rows, att_local, their_att)
    part_remote = send(part_theirs, pair_chip)

    rlo_a, rhi_a = rim_half(rim_a, fx_a, fc_a)
    from_lo_a = send(rhi_a, up_z)
    from_hi_a = send(rlo_a, down_z)
    rlo_b, rhi_b = rim_half(rim_b, fx_b, fc_b)
    from_lo_b = send(rhi_b, up_z)
    from_hi_b = send(rlo_b, down_z)

    (outputs,) = call(add_kernel, (pltpu.HBM((128, 2560), BF16),), (part, part_remote))
    done = final_half("local", own_a, fx_a, fc_a, from_lo_a, from_hi_a, dq_a)
    dk, dv, dq = final_half("remote", own_b, fx_b, fc_b, from_lo_b, from_hi_b, dq_b, *done)
    return (
        outputs.reshape(d_outputs.shape),
        dq.reshape(queries.shape),
        dk.reshape(keys.shape),
        dv.reshape(values.shape),
    )


def solution(mesh):
    spec = P("dp", "tm", "height", None, None)
    return jax.shard_map(
        body, mesh=mesh, in_specs=(spec, spec, spec, P("dp", None), spec),
        out_specs=(spec, spec, spec, spec), check_vma=False,
    )
```

```python
import functools
import math

import jax
import jax.numpy as jnp
from jax import lax
from jax.experimental import pallas as pl
from jax.experimental.pallas import tpu as pltpu
from jax.sharding import PartitionSpec as P

HDIM = 128
AXES = ("dp", "tm", "height")
NEG = -1e30
SCALE = 1.0 / math.sqrt(HDIM)
EXP2_SCALE = SCALE * math.log2(math.e)
F32 = jnp.float32
BF16 = jnp.bfloat16

HPS = 5
HPS_BWD = 5
HEADS_HALF = 10
W_HALF = 1280
VMEM_LIMIT = 10 * 1024 * 1024


def make_perm(shape, fn):
    n_dp, n_tm, n_h = shape
    pairs = []
    for d in range(n_dp):
        for t in range(n_tm):
            for h in range(n_h):
                e, u, g = fn(d, t, h)
                pairs.append(((d * n_tm + t) * n_h + h, (e * n_tm + u) * n_h + g % n_h))
    return pairs


def dot(a, b, ca, cb):
    return lax.dot_general(a, b, (((ca,), (cb,)), ((), ())), preferred_element_type=F32)


def in_vmem(shape, dtype):
    return pltpu.VMEM(shape, dtype)


def call(kernel, outs, ins, flops=0, moved=1_000_000, exps=0, scratch=(), aliases=None, hbm_in=0):
    vm = pl.BlockSpec(memory_space=pltpu.VMEM)
    hb = pl.BlockSpec(memory_space=pl.ANY)
    near = [pltpu.with_memory_space_constraint(x, pltpu.VMEM) for x in ins[: len(ins) - hbm_in]]
    far = [pltpu.with_memory_space_constraint(x, pltpu.HBM) for x in ins[len(ins) - hbm_in :]]
    out_specs = [hb if isinstance(o, jax.ShapeDtypeStruct) else vm for o in outs]
    return pl.pallas_call(
        kernel,
        out_shape=tuple(outs),
        in_specs=[vm] * len(near) + [pl.BlockSpec(memory_space=pltpu.HBM)] * len(far),
        out_specs=tuple(out_specs),
        scratch_shapes=list(scratch),
        input_output_aliases=aliases or {},
        compiler_params=pltpu.CompilerParams(vmem_limit_bytes=VMEM_LIMIT),
        cost_estimate=pl.CostEstimate(flops=flops, bytes_accessed=moved, transcendentals=exps),
    )(*near, *far)


def half_of(kind):
    mine = lax.axis_index("dp") // 4
    return mine if kind == "local" else 1 - mine


def side_rows(side, count=64):
    core = lax.axis_index("tm") % 2
    at = core * count if side == "x" else (1 - core) * count
    return pl.multiple_of(at, count)


def window_bias(zb_ref, tb_ref):
    tm = lax.axis_index("tm")
    ht = lax.axis_index("height")
    last = lax.axis_size("tm") - 1
    x_ok = jnp.where((tm > 0) & (tm < last), 1, 0)
    z_lo = jnp.where(ht > 0, 1, 0)
    z_hi = jnp.where(ht < lax.axis_size("height") - 1, 1, 0)
    q = lax.broadcasted_iota(jnp.int32, (128, 128), 0)
    k = lax.broadcasted_iota(jnp.int32, (128, 128), 1)
    late = (q // 16) % 2
    side_ok = jnp.where(late == 0, z_lo, z_hi)
    z_side = jnp.where(k < 64, 0, 1)
    zb_ref[...] = jnp.where((z_side == late) & (side_ok > 0), 0.0, NEG).astype(F32)
    t_ok = jnp.where(q < 64, x_ok, 1)
    corner = jnp.where(k < 96, 0, 1)
    t_in = (k < 64) | ((corner == late) & (side_ok > 0))
    tb_ref[...] = jnp.where(t_in & (t_ok > 0), 0.0, NEG).astype(F32)


HALOS = 10


def key_values(k_ref, v_ref, zlk_ref, zhk_ref, zlv_ref, zhv_ref, tx_ref, tc_ref, cxk_ref, cck_ref, cxv_ref, ccv_ref, c):
    cat = lambda *a: jnp.concatenate(a, axis=0)
    k_oz = cat(k_ref[:, c], zlk_ref[:, c], zhk_ref[:, c])
    v_oz = cat(v_ref[:, c], zlv_ref[:, c], zhv_ref[:, c])
    k_tx = cat(tx_ref[0, :, c], cxk_ref[:, c])
    v_tx = cat(tx_ref[1, :, c], cxv_ref[:, c])
    k_tc = cat(tc_ref[0, :, c], cck_ref[:, c])
    v_tc = cat(tc_ref[1, :, c], ccv_ref[:, c])
    return k_oz, v_oz, k_tx, v_tx, k_tc, v_tc


def both_sides(ref, c):
    return jnp.concatenate(
        [ref[pl.ds(side_rows("x"), 64), c], ref[pl.ds(side_rows("c"), 64), c]], axis=0
    )


def put_sides(ref, c, value):
    ref[pl.ds(side_rows("x"), 64), c] = value[:64]
    ref[pl.ds(side_rows("c"), 64), c] = value[64:]


def lanes(head):
    return pl.ds(pl.multiple_of(head * HDIM, HDIM), HDIM)


def forward_kernel(kind, q_ref, k_ref, v_ref, *rest):
    halo, (att_ref, p_ref, zb_ref, tb_ref) = rest[:HALOS], rest[HALOS:]
    window_bias(zb_ref, tb_ref)
    first = half_of(kind) * HEADS_HALF

    def scores(h):
        c = lanes(first + h)
        q = both_sides(q_ref, c)
        k_oz, v_oz, k_tx, v_tx, k_tc, v_tc = key_values(k_ref, v_ref, *halo, c)
        s_oz = dot(q, k_oz, 1, 1)
        s_t = jnp.concatenate([dot(q[:64], k_tx, 1, 1), dot(q[64:], k_tc, 1, 1)], axis=0)
        return s_oz, s_t, v_oz, v_tx, v_tc

    def softmax(s_oz, s_t):
        s_o = s_oz[:, :128]
        s_z = s_oz[:, 128:] + zb_ref[...]
        s_t = s_t + tb_ref[...]
        m = jnp.max(jnp.maximum(jnp.maximum(s_o, s_z), s_t), axis=1, keepdims=True)
        e_o = jnp.exp2((s_o - m) * EXP2_SCALE)
        e_z = jnp.exp2((s_z - m) * EXP2_SCALE)
        e_t = jnp.exp2((s_t - m) * EXP2_SCALE)
        inv = 1.0 / jnp.sum(e_o + e_z + e_t, axis=1, keepdims=True)
        p_oz = jnp.concatenate([e_o * inv, e_z * inv], axis=1).astype(BF16)
        return p_oz, (e_t * inv).astype(BF16)

    def attend(p_oz, p_t, v_oz, v_tx, v_tc):
        a_t = jnp.concatenate([dot(p_t[:64], v_tx, 1, 0), dot(p_t[64:], v_tc, 1, 0)], axis=0)
        return (dot(p_oz, v_oz, 1, 0) + a_t).astype(BF16)

    def step(i, carry):
        heads = [i * HPS + j for j in range(HPS)]
        scored = [scores(h) for h in heads]
        probs = [softmax(*x[:2]) for x in scored]
        att = [attend(*p, *x[2:]) for p, x in zip(probs, scored)]
        for h, (p_oz, p_t), value in zip(heads, probs, att):
            p_ref[h, :, :256] = p_oz
            p_ref[h, :, 256:] = p_t
            put_sides(att_ref, lanes(h), value)
        return carry

    lax.fori_loop(0, HEADS_HALF // HPS, step, 0)


def forward_half(kind, operands):
    return call(
        functools.partial(forward_kernel, kind),
        (in_vmem((128, W_HALF), BF16), in_vmem((HEADS_HALF, 128, 384), BF16)),
        operands, flops=2 * 2 * 10 * 128 * 384 * 128, moved=6_000_000, exps=10 * 128 * 384,
        scratch=(pltpu.VMEM((128, 128), F32), pltpu.VMEM((128, 128), F32)),
    )


def backward_kernel(kind, q_ref, k_ref, v_ref, *rest):
    halo, (p_ref, g_ref, dq_ref, own_ref, rim_ref, *t_refs) = rest[:HALOS], rest[HALOS:]
    tx_ref, cx_ref, tc_ref = t_refs
    first = half_of(kind) * HEADS_HALF

    def probs_grad(h):
        c = lanes(first + h)
        o = lanes(h)
        q = both_sides(q_ref, c)
        g = both_sides(g_ref, o)
        k_oz, v_oz, k_tx, v_tx, k_tc, v_tc = key_values(k_ref, v_ref, *halo, c)
        p_oz = p_ref[h, :, :256]
        p_t = p_ref[h, :, 256:]
        dp_oz = dot(g, v_oz, 1, 1)
        dp_t = jnp.concatenate([dot(g[:64], v_tx, 1, 1), dot(g[64:], v_tc, 1, 1)], axis=0)
        return q, g, k_oz, k_tx, k_tc, p_oz, p_t, dp_oz, dp_t

    def scores_grad(p_oz, p_t, dp_oz, dp_t):
        w_oz = p_oz.astype(F32)
        w_t = p_t.astype(F32)
        x_oz = w_oz * dp_oz
        row = jnp.sum(x_oz[:, :128] + x_oz[:, 128:] + w_t * dp_t, axis=1, keepdims=True)
        ds_oz = (w_oz * (dp_oz - row) * SCALE).astype(BF16)
        return ds_oz, (w_t * (dp_t - row) * SCALE).astype(BF16)

    def step(i, carry):
        heads = [i * HPS_BWD + j for j in range(HPS_BWD)]
        held = [probs_grad(h) for h in heads]
        values = [(dot(x[5], x[1], 0, 0), dot(x[6][:64], x[1][:64], 0, 0), dot(x[6][64:], x[1][64:], 0, 0)) for x in held]
        grads = [scores_grad(*x[5:]) for x in held]
        keys = [
            (dot(d, x[0], 0, 0), dot(t[:64], x[0][:64], 0, 0), dot(t[64:], x[0][64:], 0, 0))
            for (d, t), x in zip(grads, held)
        ]
        queries = [
            dot(d, x[2], 1, 0) + jnp.concatenate([dot(t[:64], x[3], 1, 0), dot(t[64:], x[4], 1, 0)], axis=0)
            for (d, t), x in zip(grads, held)
        ]
        for h, key, value, query in zip(heads, keys, values, queries):
            o = lanes(h)
            put_sides(dq_ref, o, query.astype(BF16))
            for kv, (d_oz, d_x, d_c) in ((0, key), (1, value)):
                own_ref[kv, :, o] = d_oz[:128]
                rim_ref[kv, :, o] = d_oz[128:]
                d_x = d_x.astype(BF16)
                tx_ref[kv, :, o] = d_x[:64]
                cx_ref[kv, :, o] = d_x[64:]
                tc_ref[kv, :, o] = d_c.astype(BF16)
        return carry

    lax.fori_loop(0, HEADS_HALF // HPS_BWD, step, 0)


def backward_half(kind, operands, probs, grad):
    pair = (2, 128, W_HALF)
    return call(
        functools.partial(backward_kernel, kind),
        (in_vmem((128, W_HALF), BF16), in_vmem(pair, F32), in_vmem(pair, F32),
         *(in_vmem((2, 64, W_HALF), BF16),) * 2, in_vmem(pair, BF16)),
        (*operands, probs, grad), flops=4 * 2 * 10 * 128 * 384 * 128, moved=12_000_000,
    )


def shard_rows(which):
    y = lax.axis_index("dp") % 4
    core = lax.axis_index("tm") % 2
    toward = jnp.where(core == 0, 3, 1)
    shard = {"own": y, "near": (y + toward) % 4, "far": (y + 4 - toward) % 4}.get(which, (y + 2) % 4)
    at = shard * 320
    if which == "c0":
        at = at + core * 160
    if which == "c1":
        at = at + (1 - core) * 160
    return at


def put_rows(dst_ref, src_ref, which):
    rows = src_ref.shape[0]
    at = shard_rows(which)

    def step(i, carry):
        r = pl.multiple_of(i * 32, 32)
        dst_ref[pl.ds(pl.multiple_of(at + r, 32), 32), :] = src_ref[pl.ds(r, 32), :]
        return carry

    lax.fori_loop(0, rows // 32, step, 0)


def gather_kernel(own_ref, near_ref, far_ref, w_ref):
    put_rows(w_ref, own_ref, "own")
    put_rows(w_ref, near_ref, "near")
    put_rows(w_ref, far_ref, "far")


def gather_rows(own, near, far):
    return call(
        gather_kernel, (in_vmem((W_HALF, 2560), BF16),), (own, near, far), moved=10_000_000
    )[0]


def grad_proj_kernel(w_in, c0_ref, c1_ref, mine_ref, theirs_ref, w_ref, o_ref, t_ref):
    put_rows(w_ref, c0_ref, "c0")
    put_rows(w_ref, c1_ref, "c1")

    def step(n, carry):
        r = pl.ds(pl.multiple_of(n * 256, 256), 256)
        w = w_ref[r, :]
        o_ref[:, r] = dot(mine_ref[...], w, 1, 1).astype(BF16)
        t_ref[:, r] = dot(theirs_ref[...], w, 1, 1).astype(BF16)
        return carry

    lax.fori_loop(0, W_HALF // 256, step, 0)


def grad_proj(w, c0, c1, mine, theirs):
    return call(
        grad_proj_kernel,
        (in_vmem((W_HALF, 2560), BF16), in_vmem((128, W_HALF), BF16), in_vmem((128, W_HALF), BF16)),
        (w, c0, c1, mine, theirs), flops=2 * 256 * 1280 * 2560, moved=9_000_000, aliases={0: 0},
    )


def out_proj_kernel(w_ref, mine_ref, theirs_ref, o_ref, t_ref):
    def step(n, carry):
        r = pl.ds(pl.multiple_of(n * 256, 256), 256)
        w = w_ref[:, r]
        o_ref[:, r] = dot(mine_ref[...], w, 1, 0)
        t_ref[:, r] = dot(theirs_ref[...], w, 1, 0).astype(BF16)
        return carry

    lax.fori_loop(0, 2560 // 256, step, 0)


def out_proj(w, mine, theirs):
    return call(
        out_proj_kernel, (in_vmem((128, 2560), F32), in_vmem((128, 2560), BF16)),
        (w, mine, theirs), flops=2 * 256 * 1280 * 2560, moved=9_000_000,
    )


def rim_kernel(rim_ref, fx_ref, fc_ref, lo_ref, hi_ref):
    for side, src, first in (("x", fx_ref, 0), ("c", fc_ref, 64)):
        at = side_rows(side, 32)
        for half, out in ((0, lo_ref), (1, hi_ref)):
            corner = src[:, first + 32 * half : first + 32 * half + 32].astype(F32)
            here = rim_ref[:, pl.ds(pl.multiple_of(64 * half + at, 32), 32)]
            out[:, pl.ds(at, 32)] = (here + corner).astype(BF16)


def rim_half(rim, from_x, from_c):
    return call(
        rim_kernel, (in_vmem((2, 64, W_HALF), BF16),) * 2, (rim, from_x, from_c),
        moved=4_000_000,
    )


def final_kernel(kind, own_ref, fx_ref, fc_ref, lo_ref, hi_ref, d_ref, *rest):
    dk_ref, dv_ref, dq_ref, dk_tile, dv_tile, sems = rest[-6:]
    at = pl.ds(pl.multiple_of(half_of(kind) * W_HALF, W_HALF), W_HALF)
    copies = [pltpu.make_async_copy(d_ref, dq_ref.at[:, at], sems.at[2])]
    copies[0].start()
    for kv, tile, out in ((0, dk_tile, dk_ref), (1, dv_tile, dv_ref)):
        for side, src in (("x", fx_ref), ("c", fc_ref)):
            for f in range(2):
                for n, z_ref in ((0, lo_ref), (1, hi_ref)):
                    r = pl.ds(pl.multiple_of(side_rows(side) + f * 32 + n * 16, 16), 16)
                    z = z_ref[kv, pl.ds(pl.multiple_of(side_rows(side, 32) + f * 16, 16), 16)]
                    t = src[kv, f * 32 + n * 16 : f * 32 + n * 16 + 16]
                    tile[r] = (own_ref[kv, r] + t.astype(F32) + z.astype(F32)).astype(BF16)
        copies.append(pltpu.make_async_copy(tile, out.at[:, at], sems.at[kv]))
        copies[-1].start()
    for cp in copies:
        cp.wait()


def final_half(kind, own, from_x, from_c, from_lo, from_hi, d_q, *earlier):
    whole = jax.ShapeDtypeStruct((128, 2560), BF16)
    return call(
        functools.partial(final_kernel, kind), (whole,) * 3,
        (own, from_x, from_c, from_lo, from_hi, d_q, *earlier), moved=6_000_000,
        scratch=(pltpu.VMEM((128, W_HALF), BF16), pltpu.VMEM((128, W_HALF), BF16), pltpu.SemaphoreType.DMA((3,))),
        aliases={6: 0, 7: 1, 8: 2} if earlier else {}, hbm_in=len(earlier),
    )


def prep_kernel(k_ref, v_ref, zlk_ref, zhk_ref, zlv_ref, zhv_ref, tx_ref, tc_ref, sems):
    copies = []
    for src, lo_ref, hi_ref in ((k_ref, zlk_ref, zhk_ref), (v_ref, zlv_ref, zhv_ref)):
        for f in range(4):
            rows = pl.ds(f * 16, 16)
            copies.append((src.at[pl.ds(f * 32 + 16, 16)], hi_ref.at[rows]))
            copies.append((src.at[pl.ds(f * 32, 16)], lo_ref.at[rows]))
    for kv, src in ((0, k_ref), (1, v_ref)):
        copies.append((src.at[pl.ds(side_rows("x"), 64)], tx_ref.at[kv]))
        copies.append((src.at[pl.ds(side_rows("c"), 64)], tc_ref.at[kv]))
    copies = [pltpu.make_async_copy(x, y, sems.at[n]) for n, (x, y) in enumerate(copies)]
    for cp in copies:
        cp.start()
    for cp in copies:
        cp.wait()


def prep(keys, values):
    return call(
        prep_kernel, (in_vmem((64, 2560), BF16),) * 4 + (in_vmem((2, 64, 2560), BF16),) * 2,
        (keys, values), moved=4_000_000, scratch=(pltpu.SemaphoreType.DMA((20,)),), hbm_in=2,
    )


def slice_kernel(near_ref, part_ref):
    core = lax.axis_index("tm") % 2

    def step(i, carry):
        r = pl.multiple_of(i * 32, 32)
        part_ref[pl.ds(r, 32), :] = near_ref[pl.ds(pl.multiple_of(core * 160 + r, 32), 32), :]
        return carry

    lax.fori_loop(0, 5, step, 0)


def add_kernel(part_ref, remote_ref, out_ref):
    out_ref[...] = (part_ref[...] + remote_ref[...].astype(F32)).astype(BF16)


def corner_kernel(lo_ref, hi_ref, cx_ref, cc_ref):
    for side, out in (("x", cx_ref), ("c", cc_ref)):
        r = pl.ds(side_rows(side, 32), 32)
        out[:32] = lo_ref[r]
        out[32:] = hi_ref[r]


def corners(z_lo, z_hi):
    return call(corner_kernel, (in_vmem((64, 2560), BF16),) * 2, (z_lo, z_hi), moved=1_300_000)


def body(queries, keys, values, projection, d_outputs):
    shape = (lax.axis_size("dp"), lax.axis_size("tm"), lax.axis_size("height"))

    def send(x, fn):
        return lax.ppermute(x, AXES, make_perm(shape, fn))

    pair_chip = lambda d, t, h: (d ^ 4, t ^ 2, h)
    other_core = lambda d, t, h: (d, t ^ 1, h)
    ring_y = lambda d, t, h: ((d & 4) | ((d + (1 if t % 2 == 0 else 3)) & 3), t, h)
    up_z = lambda d, t, h: (d, t, h + 1)
    down_z = lambda d, t, h: (d, t, h - 1)
    other_chip = lambda d, t, h: (d, 3 - t, h) if t in (1, 2) else (d ^ 4, 3 - t, h)
    other_chip_mid = lambda d, t, h: (d, 3 - t, h) if t in (1, 2) else (d, t, h ^ 1)
    other_chip_late = lambda d, t, h: (d, 3 - t, h) if t in (1, 2) else (d ^ 1, t, h)

    tokens = queries.shape[1] * queries.shape[2] * queries.shape[3]
    flat = lambda a: a.reshape(tokens, a.shape[-1])
    q, k, v, d_out = flat(queries), flat(keys), flat(values), flat(d_outputs)

    w_near = send(projection, ring_y)
    their_d_out = send(d_out, pair_chip)
    k_lo_s, k_hi_s, v_lo_s, v_hi_s, tx_s, tc_s = prep(k, v)
    k_lo = send(k_hi_s, up_z)
    k_hi = send(k_lo_s, down_z)
    v_lo = send(v_hi_s, up_z)
    v_hi = send(v_lo_s, down_z)
    t_x = send(tx_s, other_chip)
    t_c = send(tc_s, other_core)
    cxk_s, cck_s = corners(k_lo, k_hi)
    cxk = send(cxk_s, other_chip)
    cck = send(cck_s, other_core)
    cxv_s, ccv_s = corners(v_lo, v_hi)
    cxv = send(cxv_s, other_chip_mid)
    ccv = send(ccv_s, other_core)
    w_far = send(w_near, other_core)
    (w_part,) = call(slice_kernel, (in_vmem((160, 2560), BF16),), (w_near,))
    w_c0 = send(w_part, ring_y)
    w_c1 = send(w_c0, other_core)
    rows = gather_rows(projection, w_near, w_far)

    operands = (q, k, v, k_lo, k_hi, v_lo, v_hi, t_x, t_c, cxk, cck, cxv, ccv)
    att_remote, p_remote = forward_half("remote", operands)
    their_att = send(att_remote, pair_chip)
    att_local, p_local = forward_half("local", operands)

    rows, g_local, g_theirs = grad_proj(rows, w_c0, w_c1, d_out, their_d_out)
    g_remote = send(g_theirs, pair_chip)

    dq_a, own_a, rim_a, tx_a, cx_a, tc_a = backward_half("local", operands, p_local, g_local)
    ex_a = send(cx_a, other_chip_late)
    fx_a = send(tx_a, other_chip_late)
    fc_a = send(tc_a, other_core)
    dq_b, own_b, rim_b, tx_b, cx_b, tc_b = backward_half("remote", operands, p_remote, g_remote)
    ex_b = send(cx_b, other_chip_late)
    fx_b = send(tx_b, other_chip_late)
    fc_b = send(tc_b, other_core)

    part, part_theirs = out_proj(rows, att_local, their_att)
    part_remote = send(part_theirs, pair_chip)

    rlo_a, rhi_a = rim_half(rim_a, ex_a, fc_a)
    from_lo_a = send(rhi_a, up_z)
    from_hi_a = send(rlo_a, down_z)
    rlo_b, rhi_b = rim_half(rim_b, ex_b, fc_b)
    from_lo_b = send(rhi_b, up_z)
    from_hi_b = send(rlo_b, down_z)

    (outputs,) = call(add_kernel, (pltpu.HBM((128, 2560), BF16),), (part, part_remote))
    done = final_half("local", own_a, fx_a, fc_a, from_lo_a, from_hi_a, dq_a)
    dk, dv, dq = final_half("remote", own_b, fx_b, fc_b, from_lo_b, from_hi_b, dq_b, *done)
    return (
        outputs.reshape(d_outputs.shape),
        dq.reshape(queries.shape),
        dk.reshape(keys.shape),
        dv.reshape(values.shape),
    )


def solution(mesh):
    spec = P("dp", "tm", "height", None, None)
    return jax.shard_map(
        body, mesh=mesh, in_specs=(spec, spec, spec, P("dp", None), spec),
        out_specs=(spec, spec, spec, spec), check_vma=False,
    )
```

```python
import functools
import math

import jax
import jax.numpy as jnp
from jax import lax
from jax.experimental import pallas as pl
from jax.experimental.pallas import tpu as pltpu
from jax.sharding import PartitionSpec as P

HDIM = 128
AXES = ("dp", "tm", "height")
NEG = -1e30
SCALE = 1.0 / math.sqrt(HDIM)
EXP2_SCALE = SCALE * math.log2(math.e)
F32 = jnp.float32
BF16 = jnp.bfloat16

HPS = 5
HPS_BWD = 5
HEADS_HALF = 10
W_HALF = 1280
VMEM_LIMIT = 10 * 1024 * 1024


def make_perm(shape, fn):
    n_dp, n_tm, n_h = shape
    pairs = []
    for d in range(n_dp):
        for t in range(n_tm):
            for h in range(n_h):
                to = fn(d, t, h)
                if to is not None:
                    e, u, g = to
                    pairs.append(((d * n_tm + t) * n_h + h, (e * n_tm + u) * n_h + g % n_h))
    return pairs


def dot(a, b, ca, cb):
    return lax.dot_general(a, b, (((ca,), (cb,)), ((), ())), preferred_element_type=F32)


def in_vmem(shape, dtype):
    return pltpu.VMEM(shape, dtype)


def call(kernel, outs, ins, flops=0, moved=1_000_000, exps=0, scratch=(), aliases=None, hbm_in=0):
    vm = pl.BlockSpec(memory_space=pltpu.VMEM)
    hb = pl.BlockSpec(memory_space=pl.ANY)
    near = [pltpu.with_memory_space_constraint(x, pltpu.VMEM) for x in ins[: len(ins) - hbm_in]]
    far = [pltpu.with_memory_space_constraint(x, pltpu.HBM) for x in ins[len(ins) - hbm_in :]]
    out_specs = [hb if isinstance(o, jax.ShapeDtypeStruct) else vm for o in outs]
    return pl.pallas_call(
        kernel,
        out_shape=tuple(outs),
        in_specs=[vm] * len(near) + [pl.BlockSpec(memory_space=pltpu.HBM)] * len(far),
        out_specs=tuple(out_specs),
        scratch_shapes=list(scratch),
        input_output_aliases=aliases or {},
        compiler_params=pltpu.CompilerParams(vmem_limit_bytes=VMEM_LIMIT),
        cost_estimate=pl.CostEstimate(flops=flops, bytes_accessed=moved, transcendentals=exps),
    )(*near, *far)


def half_of(kind):
    mine = lax.axis_index("dp") // 4
    return mine if kind == "local" else 1 - mine


def side_rows(side, count=64):
    core = lax.axis_index("tm") % 2
    at = core * count if side == "x" else (1 - core) * count
    return pl.multiple_of(at, count)


def window_bias(zb_ref, tb_ref):
    tm = lax.axis_index("tm")
    ht = lax.axis_index("height")
    last = lax.axis_size("tm") - 1
    x_ok = jnp.where((tm > 0) & (tm < last), 1, 0)
    z_lo = jnp.where(ht > 0, 1, 0)
    z_hi = jnp.where(ht < lax.axis_size("height") - 1, 1, 0)
    q = lax.broadcasted_iota(jnp.int32, (128, 128), 0)
    k = lax.broadcasted_iota(jnp.int32, (128, 128), 1)
    late = (q // 16) % 2
    side_ok = jnp.where(late == 0, z_lo, z_hi)
    z_side = jnp.where(k < 64, 0, 1)
    zb_ref[...] = jnp.where((z_side == late) & (side_ok > 0), 0.0, NEG).astype(F32)
    t_ok = jnp.where(q < 64, x_ok, 1)
    corner = jnp.where(k < 96, 0, 1)
    t_in = (k < 64) | ((corner == late) & (side_ok > 0))
    tb_ref[...] = jnp.where(t_in & (t_ok > 0), 0.0, NEG).astype(F32)


HALOS = 10


def key_values(k_ref, v_ref, zlk_ref, zhk_ref, zlv_ref, zhv_ref, tx_ref, tc_ref, cxk_ref, cck_ref, cxv_ref, ccv_ref, c):
    cat = lambda *a: jnp.concatenate(a, axis=0)
    k_oz = cat(k_ref[:, c], zlk_ref[:, c], zhk_ref[:, c])
    v_oz = cat(v_ref[:, c], zlv_ref[:, c], zhv_ref[:, c])
    k_tx = cat(tx_ref[0, :, c], cxk_ref[:, c])
    v_tx = cat(tx_ref[1, :, c], cxv_ref[:, c])
    k_tc = cat(tc_ref[0, :, c], cck_ref[:, c])
    v_tc = cat(tc_ref[1, :, c], ccv_ref[:, c])
    return k_oz, v_oz, k_tx, v_tx, k_tc, v_tc


def both_sides(ref, c):
    return jnp.concatenate(
        [ref[pl.ds(side_rows("x"), 64), c], ref[pl.ds(side_rows("c"), 64), c]], axis=0
    )


def put_sides(ref, c, value):
    ref[pl.ds(side_rows("x"), 64), c] = value[:64]
    ref[pl.ds(side_rows("c"), 64), c] = value[64:]


def lanes(head):
    return pl.ds(pl.multiple_of(head * HDIM, HDIM), HDIM)


def forward_kernel(kind, q_ref, k_ref, v_ref, *rest):
    halo, (att_ref, p_ref, zb_ref, tb_ref) = rest[:HALOS], rest[HALOS:]
    window_bias(zb_ref, tb_ref)
    first = half_of(kind) * HEADS_HALF

    def scores(h):
        c = lanes(first + h)
        q = both_sides(q_ref, c)
        k_oz, v_oz, k_tx, v_tx, k_tc, v_tc = key_values(k_ref, v_ref, *halo, c)
        s_oz = dot(q, k_oz, 1, 1)
        s_t = jnp.concatenate([dot(q[:64], k_tx, 1, 1), dot(q[64:], k_tc, 1, 1)], axis=0)
        return s_oz, s_t, v_oz, v_tx, v_tc

    def softmax(s_oz, s_t):
        s_o = s_oz[:, :128]
        s_z = s_oz[:, 128:] + zb_ref[...]
        s_t = s_t + tb_ref[...]
        m = jnp.max(jnp.maximum(jnp.maximum(s_o, s_z), s_t), axis=1, keepdims=True)
        e_o = jnp.exp2((s_o - m) * EXP2_SCALE)
        e_z = jnp.exp2((s_z - m) * EXP2_SCALE)
        e_t = jnp.exp2((s_t - m) * EXP2_SCALE)
        inv = 1.0 / jnp.sum(e_o + e_z + e_t, axis=1, keepdims=True)
        p_oz = jnp.concatenate([e_o * inv, e_z * inv], axis=1).astype(BF16)
        return p_oz, (e_t * inv).astype(BF16)

    def attend(p_oz, p_t, v_oz, v_tx, v_tc):
        a_t = jnp.concatenate([dot(p_t[:64], v_tx, 1, 0), dot(p_t[64:], v_tc, 1, 0)], axis=0)
        return (dot(p_oz, v_oz, 1, 0) + a_t).astype(BF16)

    def step(i, carry):
        heads = [i * HPS + j for j in range(HPS)]
        scored = [scores(h) for h in heads]
        probs = [softmax(*x[:2]) for x in scored]
        att = [attend(*p, *x[2:]) for p, x in zip(probs, scored)]
        for h, (p_oz, p_t), value in zip(heads, probs, att):
            p_ref[h, :, :256] = p_oz
            p_ref[h, :, 256:] = p_t
            put_sides(att_ref, lanes(h), value)
        return carry

    lax.fori_loop(0, HEADS_HALF // HPS, step, 0)


def forward_half(kind, operands):
    return call(
        functools.partial(forward_kernel, kind),
        (in_vmem((128, W_HALF), BF16), in_vmem((HEADS_HALF, 128, 384), BF16)),
        operands, flops=2 * 2 * 10 * 128 * 384 * 128, moved=6_000_000, exps=10 * 128 * 384,
        scratch=(pltpu.VMEM((128, 128), F32), pltpu.VMEM((128, 128), F32)),
    )


def backward_kernel(kind, q_ref, k_ref, v_ref, *rest):
    halo, (p_ref, g_ref, dq_ref, own_ref, rim_ref, *t_refs) = rest[:HALOS], rest[HALOS:]
    tx_ref, cx_ref, tc_ref = t_refs
    first = half_of(kind) * HEADS_HALF

    def probs_grad(h):
        c = lanes(first + h)
        o = lanes(h)
        q = both_sides(q_ref, c)
        g = both_sides(g_ref, o)
        k_oz, v_oz, k_tx, v_tx, k_tc, v_tc = key_values(k_ref, v_ref, *halo, c)
        p_oz = p_ref[h, :, :256]
        p_t = p_ref[h, :, 256:]
        dp_oz = dot(g, v_oz, 1, 1)
        dp_t = jnp.concatenate([dot(g[:64], v_tx, 1, 1), dot(g[64:], v_tc, 1, 1)], axis=0)
        return q, g, k_oz, k_tx, k_tc, p_oz, p_t, dp_oz, dp_t

    def scores_grad(p_oz, p_t, dp_oz, dp_t):
        w_oz = p_oz.astype(F32)
        w_t = p_t.astype(F32)
        x_oz = w_oz * dp_oz
        row = jnp.sum(x_oz[:, :128] + x_oz[:, 128:] + w_t * dp_t, axis=1, keepdims=True)
        ds_oz = (w_oz * (dp_oz - row) * SCALE).astype(BF16)
        return ds_oz, (w_t * (dp_t - row) * SCALE).astype(BF16)

    def step(i, carry):
        heads = [i * HPS_BWD + j for j in range(HPS_BWD)]
        held = [probs_grad(h) for h in heads]
        values = [(dot(x[5], x[1], 0, 0), dot(x[6][:64], x[1][:64], 0, 0), dot(x[6][64:], x[1][64:], 0, 0)) for x in held]
        grads = [scores_grad(*x[5:]) for x in held]
        keys = [
            (dot(d, x[0], 0, 0), dot(t[:64], x[0][:64], 0, 0), dot(t[64:], x[0][64:], 0, 0))
            for (d, t), x in zip(grads, held)
        ]
        queries = [
            dot(d, x[2], 1, 0) + jnp.concatenate([dot(t[:64], x[3], 1, 0), dot(t[64:], x[4], 1, 0)], axis=0)
            for (d, t), x in zip(grads, held)
        ]
        for h, key, value, query in zip(heads, keys, values, queries):
            o = lanes(h)
            put_sides(dq_ref, o, query.astype(BF16))
            for kv, (d_oz, d_x, d_c) in ((0, key), (1, value)):
                own_ref[kv, :, o] = d_oz[:128]
                rim_ref[kv, :, o] = d_oz[128:]
                d_x = d_x.astype(BF16)
                tx_ref[kv, :, o] = d_x[:64]
                cx_ref[kv, :, o] = d_x[64:]
                tc_ref[kv, :, o] = d_c.astype(BF16)
        return carry

    lax.fori_loop(0, HEADS_HALF // HPS_BWD, step, 0)


def backward_half(kind, operands, probs, grad):
    pair = (2, 128, W_HALF)
    return call(
        functools.partial(backward_kernel, kind),
        (in_vmem((128, W_HALF), BF16), in_vmem(pair, F32), in_vmem(pair, F32),
         *(in_vmem((2, 64, W_HALF), BF16),) * 2, in_vmem(pair, BF16)),
        (*operands, probs, grad), flops=4 * 2 * 10 * 128 * 384 * 128, moved=12_000_000,
    )


def shard_rows(which):
    y = lax.axis_index("dp") % 4
    core = lax.axis_index("tm") % 2
    toward = jnp.where(core == 0, 3, 1)
    shard = {"own": y, "near": (y + toward) % 4, "far": (y + 4 - toward) % 4, "c": (y + 2) % 4}
    name, part = (which + ":").split(":")[:2]
    return shard[name] * 320 + {"": 0, "same": core * 160, "other": (1 - core) * 160}[part]


def put_rows(dst_ref, src_ref, which):
    rows = src_ref.shape[0]
    at = shard_rows(which)

    def step(i, carry):
        r = pl.multiple_of(i * 32, 32)
        dst_ref[pl.ds(pl.multiple_of(at + r, 32), 32), :] = src_ref[pl.ds(r, 32), :]
        return carry

    lax.fori_loop(0, rows // 32, step, 0)


def gather_kernel(own_ref, na_ref, nb_ref, fa_ref, fb_ref, w_ref):
    put_rows(w_ref, own_ref, "own")
    put_rows(w_ref, na_ref, "near:same")
    put_rows(w_ref, nb_ref, "near:other")
    put_rows(w_ref, fa_ref, "far:other")
    put_rows(w_ref, fb_ref, "far:same")


def gather_rows(*parts):
    return call(gather_kernel, (in_vmem((W_HALF, 2560), BF16),), parts, moved=10_000_000)[0]


def grad_proj_kernel(w_in, c0_ref, c1_ref, mine_ref, theirs_ref, w_ref, o_ref, t_ref):
    put_rows(w_ref, c0_ref, "c:same")
    put_rows(w_ref, c1_ref, "c:other")

    def step(n, carry):
        r = pl.ds(pl.multiple_of(n * 256, 256), 256)
        w = w_ref[r, :]
        o_ref[:, r] = dot(mine_ref[...], w, 1, 1).astype(BF16)
        t_ref[:, r] = dot(theirs_ref[...], w, 1, 1).astype(BF16)
        return carry

    lax.fori_loop(0, W_HALF // 256, step, 0)


def grad_proj(w, c0, c1, mine, theirs):
    return call(
        grad_proj_kernel,
        (in_vmem((W_HALF, 2560), BF16), in_vmem((128, W_HALF), BF16), in_vmem((128, W_HALF), BF16)),
        (w, c0, c1, mine, theirs), flops=2 * 256 * 1280 * 2560, moved=9_000_000, aliases={0: 0},
    )


def out_proj_kernel(w_ref, mine_ref, theirs_ref, o_ref, t_ref):
    def step(n, carry):
        r = pl.ds(pl.multiple_of(n * 256, 256), 256)
        w = w_ref[:, r]
        o_ref[:, r] = dot(mine_ref[...], w, 1, 0)
        t_ref[:, r] = dot(theirs_ref[...], w, 1, 0).astype(BF16)
        return carry

    lax.fori_loop(0, 2560 // 256, step, 0)


def out_proj(w, mine, theirs):
    return call(
        out_proj_kernel, (in_vmem((128, 2560), F32), in_vmem((128, 2560), BF16)),
        (w, mine, theirs), flops=2 * 256 * 1280 * 2560, moved=9_000_000,
    )


def rim_kernel(rim_ref, fx_ref, fc_ref, lo_ref, hi_ref):
    for side, src, first in (("x", fx_ref, 0), ("c", fc_ref, 64)):
        at = side_rows(side, 32)
        for half, out in ((0, lo_ref), (1, hi_ref)):
            corner = src[:, first + 32 * half : first + 32 * half + 32].astype(F32)
            here = rim_ref[:, pl.ds(pl.multiple_of(64 * half + at, 32), 32)]
            out[:, pl.ds(at, 32)] = (here + corner).astype(BF16)


def rim_half(rim, from_x, from_c):
    return call(
        rim_kernel, (in_vmem((2, 64, W_HALF), BF16),) * 2, (rim, from_x, from_c),
        moved=4_000_000,
    )


def final_kernel(kind, own_ref, fx_ref, fc_ref, lo_ref, hi_ref, d_ref, *rest):
    dk_ref, dv_ref, dq_ref, dk_tile, dv_tile, sems = rest[-6:]
    at = pl.ds(pl.multiple_of(half_of(kind) * W_HALF, W_HALF), W_HALF)
    copies = [pltpu.make_async_copy(d_ref, dq_ref.at[:, at], sems.at[2])]
    copies[0].start()
    for kv, tile, out in ((0, dk_tile, dk_ref), (1, dv_tile, dv_ref)):
        for side, src in (("x", fx_ref), ("c", fc_ref)):
            for f in range(2):
                for n, z_ref in ((0, lo_ref), (1, hi_ref)):
                    r = pl.ds(pl.multiple_of(side_rows(side) + f * 32 + n * 16, 16), 16)
                    z = z_ref[kv, pl.ds(pl.multiple_of(side_rows(side, 32) + f * 16, 16), 16)]
                    t = src[kv, f * 32 + n * 16 : f * 32 + n * 16 + 16]
                    tile[r] = (own_ref[kv, r] + t.astype(F32) + z.astype(F32)).astype(BF16)
        copies.append(pltpu.make_async_copy(tile, out.at[:, at], sems.at[kv]))
        copies[-1].start()
    for cp in copies:
        cp.wait()


def final_half(kind, own, from_x, from_c, from_lo, from_hi, d_q, *earlier):
    whole = jax.ShapeDtypeStruct((128, 2560), BF16)
    return call(
        functools.partial(final_kernel, kind), (whole,) * 3,
        (own, from_x, from_c, from_lo, from_hi, d_q, *earlier), moved=6_000_000,
        scratch=(pltpu.VMEM((128, W_HALF), BF16), pltpu.VMEM((128, W_HALF), BF16), pltpu.SemaphoreType.DMA((3,))),
        aliases={6: 0, 7: 1, 8: 2} if earlier else {}, hbm_in=len(earlier),
    )


def run_copies(pairs, sems):
    copies = [pltpu.make_async_copy(x, y, sems.at[n]) for n, (x, y) in enumerate(pairs)]
    for cp in copies:
        cp.start()
    for cp in copies:
        cp.wait()


def row_halo(src, lo_ref, hi_ref):
    pairs = []
    for f in range(4):
        rows = pl.ds(f * 16, 16)
        pairs.append((src.at[pl.ds(f * 32 + 16, 16)], hi_ref.at[rows]))
        pairs.append((src.at[pl.ds(f * 32, 16)], lo_ref.at[rows]))
    return pairs


def prep_k_kernel(w_ref, k_ref, wa_ref, wb_ref, lo_ref, hi_ref, sems):
    core = lax.axis_index("tm") % 2
    same = pl.ds(pl.multiple_of(core * 160, 160), 160)
    other = pl.ds(pl.multiple_of((1 - core) * 160, 160), 160)
    cut = [(w_ref.at[same], wa_ref), (w_ref.at[other], wb_ref)]
    run_copies(row_halo(k_ref, lo_ref, hi_ref) + cut, sems)


def prep_v_kernel(k_ref, v_ref, lo_ref, hi_ref, tx_ref, tc_ref, sems):
    pairs = row_halo(v_ref, lo_ref, hi_ref)
    for kv, src in ((0, k_ref), (1, v_ref)):
        pairs.append((src.at[pl.ds(side_rows("x"), 64)], tx_ref.at[kv]))
        pairs.append((src.at[pl.ds(side_rows("c"), 64)], tc_ref.at[kv]))
    run_copies(pairs, sems)


def prep(kernel, first, shapes, sources):
    return call(
        kernel, tuple(in_vmem(x, BF16) for x in (*first, *shapes)), sources, moved=3_000_000,
        scratch=(pltpu.SemaphoreType.DMA((12,)),), hbm_in=2,
    )


def add_kernel(part_ref, remote_ref, out_ref):
    out_ref[...] = (part_ref[...] + remote_ref[...].astype(F32)).astype(BF16)


def corner_kernel(lo_ref, hi_ref, cx_ref, cc_ref):
    for side, out in (("x", cx_ref), ("c", cc_ref)):
        r = pl.ds(side_rows(side, 32), 32)
        out[:32] = lo_ref[r]
        out[32:] = hi_ref[r]


def corners(z_lo, z_hi):
    return call(corner_kernel, (in_vmem((64, 2560), BF16),) * 2, (z_lo, z_hi), moved=1_300_000)


def body(queries, keys, values, projection, d_outputs):
    shape = (lax.axis_size("dp"), lax.axis_size("tm"), lax.axis_size("height"))

    def send(x, fn):
        return lax.ppermute(x, AXES, make_perm(shape, fn))

    pair_chip = lambda d, t, h: (d ^ 4, t ^ 2, h)
    other_core = lambda d, t, h: (d, t ^ 1, h)
    ring_y = lambda d, t, h: ((d & 4) | ((d + (1 if t % 2 == 0 else 3)) & 3), t, h)
    up_z = lambda d, t, h: (d, t, h + 1)
    down_z = lambda d, t, h: (d, t, h - 1)
    other_chip = lambda d, t, h: (d, 3 - t, h) if t in (1, 2) else (d ^ 4, 3 - t, h)
    middle_chip = lambda d, t, h: (d, 3 - t, h) if t in (1, 2) else None
    other_chip_mid = lambda d, t, h: (d, 3 - t, h) if t in (1, 2) else (d, t, h ^ 1)
    other_chip_late = lambda d, t, h: (d, 3 - t, h) if t in (1, 2) else (d ^ 1, t, h)

    tokens = queries.shape[1] * queries.shape[2] * queries.shape[3]
    flat = lambda a: a.reshape(tokens, a.shape[-1])
    q, k, v, d_out = flat(queries), flat(keys), flat(values), flat(d_outputs)

    half_row = ((64, 2560),) * 2
    wa_s, wb_s, k_lo_s, k_hi_s = prep(prep_k_kernel, ((160, 2560),) * 2, half_row, (projection, k))
    v_lo_s, v_hi_s, tx_s, tc_s = prep(prep_v_kernel, half_row, ((2, 64, 2560),) * 2, (k, v))
    near_a = send(wa_s, ring_y)
    near_b = send(wb_s, ring_y)
    their_d_out = send(d_out, pair_chip)
    k_lo = send(k_hi_s, up_z)
    k_hi = send(k_lo_s, down_z)
    v_lo = send(v_hi_s, up_z)
    v_hi = send(v_lo_s, down_z)
    t_x = send(tx_s, middle_chip)
    t_c = send(tc_s, other_core)
    cxk_s, cck_s = corners(k_lo, k_hi)
    cxk = send(cxk_s, other_chip)
    cck = send(cck_s, other_core)
    cxv_s, ccv_s = corners(v_lo, v_hi)
    cxv = send(cxv_s, other_chip_mid)
    ccv = send(ccv_s, other_core)
    far_a = send(near_a, other_core)
    far_b = send(near_b, other_core)
    w_c0 = send(near_a, ring_y)
    w_c1 = send(w_c0, other_core)
    rows = gather_rows(projection, near_a, near_b, far_a, far_b)

    operands = (q, k, v, k_lo, k_hi, v_lo, v_hi, t_x, t_c, cxk, cck, cxv, ccv)
    att_remote, p_remote = forward_half("remote", operands)
    their_att = send(att_remote, pair_chip)
    att_local, p_local = forward_half("local", operands)

    rows, g_local, g_theirs = grad_proj(rows, w_c0, w_c1, d_out, their_d_out)
    g_remote = send(g_theirs, pair_chip)

    dq_a, own_a, rim_a, tx_a, cx_a, tc_a = backward_half("local", operands, p_local, g_local)
    ex_a = send(cx_a, other_chip_late)
    fx_a = send(tx_a, other_chip_late)
    fc_a = send(tc_a, other_core)
    dq_b, own_b, rim_b, tx_b, cx_b, tc_b = backward_half("remote", operands, p_remote, g_remote)
    ex_b = send(cx_b, other_chip_late)
    fx_b = send(tx_b, other_chip_late)
    fc_b = send(tc_b, other_core)

    part, part_theirs = out_proj(rows, att_local, their_att)
    part_remote = send(part_theirs, pair_chip)

    rlo_a, rhi_a = rim_half(rim_a, ex_a, fc_a)
    from_lo_a = send(rhi_a, up_z)
    from_hi_a = send(rlo_a, down_z)
    rlo_b, rhi_b = rim_half(rim_b, ex_b, fc_b)
    from_lo_b = send(rhi_b, up_z)
    from_hi_b = send(rlo_b, down_z)

    (outputs,) = call(add_kernel, (pltpu.HBM((128, 2560), BF16),), (part, part_remote))
    done = final_half("local", own_a, fx_a, fc_a, from_lo_a, from_hi_a, dq_a)
    dk, dv, dq = final_half("remote", own_b, fx_b, fc_b, from_lo_b, from_hi_b, dq_b, *done)
    return (
        outputs.reshape(d_outputs.shape),
        dq.reshape(queries.shape),
        dk.reshape(keys.shape),
        dv.reshape(values.shape),
    )


def solution(mesh):
    spec = P("dp", "tm", "height", None, None)
    return jax.shard_map(
        body, mesh=mesh, in_specs=(spec, spec, spec, P("dp", None), spec),
        out_specs=(spec, spec, spec, spec), check_vma=False,
    )
```
